1024 devices in a mesh: frames: 16 (over x_hi, y, core), rows: 64 (over x_lo, z).
Axes of the slice: x: 4 (x_hi: 2, x_lo: 2; x = x_hi * 2 + x_lo), y: 4, z: 32, core: 2. Of those that a mesh axis runs over, the one named last changes fastest.
Arguments:
- fine_q: bfloat16 [16, 512, 16, 256], P('frames', 'rows'), may hold values from -24 to 24
- fine_kv: bfloat16 [16, 512, 16, 512], P('frames', 'rows'), may hold values from -24 to 24
- coarse_q: bfloat16 [16, 64, 2, 1024], P('frames', 'rows'), may hold values from -24 to 24
- coarse_kv: bfloat16 [16, 64, 2, 2048], P('frames', 'rows'), may hold values from -24 to 24
- cotangent: bfloat16 [16, 512, 16, 256], P('frames', 'rows'), may hold values from -6 to 6
- gain_table: float32 [1000, 256], replicated, may hold values from 0.3 to 3
- timesteps: int32 [16], P('frames'), may hold values from 0 to 999
- valid_cols: int32 [16], replicated, may hold values from 8 to 16
Outputs:
- grad_fine_q: bfloat16 [16, 512, 16, 256], P('frames', 'rows')
- grad_fine_kv: bfloat16 [16, 512, 16, 512], P('frames', 'rows')
- grad_coarse_q: bfloat16 [16, 64, 2, 1024], P(None, 'rows', None, 'frames')
- grad_coarse_k: bfloat16 [16, 64, 2, 1024], P(None, 'rows', None, 'frames')
- grad_coarse_v: bfloat16 [16, 64, 2, 1024], P(None, 'rows', None, 'frames')
The draws below stay inside these ranges and needn't reach their ends.
All inputs are finite; a program needn't handle non-finite values.
Results may differ from the reference program's by a relative error of at most 0.023.
Values may be sent and summed in bfloat16 or wider, within the bound.
A program may use at most 32 MiB of HBM per device.

```python
import math
import jax
import jax.numpy as jnp
from jax import lax

HD = 64
FINE_HEADS = 4
FWIDTH = 256
CWIDTH = 1024
KERNEL = 7
POOL = 8
STEPS = 1000
WIDTH = 16
FRAMES = 16
HEIGHT = 512
CROWS = 64
CCOLS = 2


def drawn(key, dims, query_spread):
    root_key = jax.random.fold_in(key, 7)
    key_query = jax.random.fold_in(root_key, 1)
    key_vectors = jax.random.fold_in(root_key, 2)
    key_values = jax.random.fold_in(root_key, 3)
    query = jax.random.normal(key_query, dims, jnp.float32) * query_spread
    vectors = jax.random.normal(key_vectors, dims, jnp.float32)
    values = jax.random.normal(key_values, dims, jnp.float32)
    query = jnp.clip(query, -24.0, 24.0)
    vectors = jnp.clip(vectors, -24.0, 24.0)
    values = jnp.clip(values, -24.0, 24.0)
    return (query, vectors, values)


def fine_draw(key):
    return drawn(key, (FRAMES, HEIGHT, WIDTH, FINE_HEADS, HD), 1.0)


def coarse_draw(key):
    return drawn(key, (FRAMES, CROWS, CCOLS, CWIDTH // HD, HD), 2.0)


def draw_fine_q(key, part):
    query, vectors, values = fine_draw(key)
    return query.reshape(FRAMES, HEIGHT, WIDTH, FWIDTH).astype(jnp.bfloat16)


def draw_fine_kv(key, part):
    query, vectors, values = fine_draw(key)
    joined = jnp.concatenate([vectors.reshape(FRAMES, HEIGHT, WIDTH, FWIDTH), values.reshape(FRAMES, HEIGHT, WIDTH, FWIDTH)], axis=-1)
    return joined.astype(jnp.bfloat16)


def draw_coarse_q(key, part):
    query, vectors, values = coarse_draw(key)
    return query.reshape(FRAMES, CROWS, CCOLS, CWIDTH).astype(jnp.bfloat16)


def draw_coarse_kv(key, part):
    query, vectors, values = coarse_draw(key)
    joined = jnp.concatenate([vectors.reshape(FRAMES, CROWS, CCOLS, CWIDTH), values.reshape(FRAMES, CROWS, CCOLS, CWIDTH)], axis=-1)
    return joined.astype(jnp.bfloat16)


def plant(result, own_key, smallest, top_value):
    spot = [jax.random.randint(jax.random.fold_in(own_key, axis), (), 0, length) for axis, length in enumerate(result.shape)]
    longest = result.shape.index(max(result.shape))
    next_to = spot[:longest] + [(spot[longest] + 1) % result.shape[longest]] + spot[longest + 1:]
    return result.at[tuple(spot)].set(smallest).at[tuple(next_to)].set(top_value)


def steps_of(rng, shape, cuts, smallest, high):
    def one(dim, blocks):
        steps = jax.random.uniform(jax.random.fold_in(jax.random.fold_in(rng, 6), dim), (blocks,), jnp.float32, smallest / len(cuts), high / len(cuts))
        return jnp.repeat(jnp.exp(steps), shape[dim] // blocks).reshape((-1,) + (1,) * (len(shape) - dim - 1))

    level = one(*cuts[0])
    for cut in cuts[1:]:
        level = level * one(*cut)
    return level


def bell_draw(own_key, shape, spread, reach, cuts=(), kind=jnp.bfloat16):
    gain = steps_of(own_key, shape, cuts, -0.22, 0.18) if cuts else 1.0
    drawn = jax.random.normal(own_key, shape, jnp.float32) * spread * gain
    return jnp.minimum(jnp.maximum(drawn, -reach), reach).astype(kind)


def setup_inputs(seed: int = 0) -> dict:
    splits = jax.random.split(jax.random.key(seed), 9)
    fine_q = draw_fine_q(jax.random.fold_in(splits[8], 71), 0)
    fine_kv = draw_fine_kv(jax.random.fold_in(splits[8], 71), 0)
    coarse_q = draw_coarse_q(jax.random.fold_in(splits[8], 71), 0)
    coarse_kv = draw_coarse_kv(jax.random.fold_in(splits[8], 71), 0)
    cotangent = bell_draw(splits[4], (FRAMES, HEIGHT, WIDTH, FWIDTH), 1.0, 6.0, ((0, 16), (1, 64)))
    gain_table = jnp.clip(jnp.exp(jax.random.uniform(splits[5], (STEPS, FWIDTH), jnp.float32, math.log(0.3), math.log(3.0))), 0.3, 3.0)
    timesteps = plant(jax.random.randint(splits[6], (FRAMES,), 0, STEPS), jax.random.fold_in(splits[6], 1), 0, STEPS - 1).astype(jnp.int32)
    valid_cols = plant(jax.random.randint(splits[7], (FRAMES,), WIDTH // 2, WIDTH + 1), jax.random.fold_in(splits[7], 1), WIDTH // 2, WIDTH).astype(jnp.int32)
    return dict(fine_q=fine_q, fine_kv=fine_kv, coarse_q=coarse_q, coarse_kv=coarse_kv, cotangent=cotangent, gain_table=gain_table, timesteps=timesteps, valid_cols=valid_cols)


NEGATIVE = -1e+30

def lowered(value):
    return lax.optimization_barrier(value.astype(jnp.bfloat16)).astype(jnp.float32)

def fine_frame(record):
    query, key_value, grad, valid = record
    height, width, fine_width = query.shape
    head_count = fine_width // HD
    radius = KERNEL // 2
    score_scale = 1.0 / math.sqrt(HD)
    query_wide = query.astype(jnp.float32).reshape(height, width, head_count, HD)
    padded = jnp.pad(key_value.astype(jnp.float32), ((radius, radius), (radius, radius), (0, 0)))
    key_table = padded[..., :fine_width].reshape(height + 2 * radius, width + 2 * radius, head_count, HD)
    value_table = padded[..., fine_width:].reshape(height + 2 * radius, width + 2 * radius, head_count, HD)
    grad_table = lowered(grad).reshape(height, width, head_count, HD)
    row_ids = jnp.arange(height)[:, None]
    col_ids = jnp.arange(width)[None, :]
    offsets = [(row_step, col_step) for row_step in range(-radius, radius + 1) for col_step in range(-radius, radius + 1)]

    def shifted(table, row_step, col_step):
        return table[radius + row_step:radius + row_step + height, radius + col_step:radius + col_step + width]
    score_list = []
    for row_step, col_step in offsets:
        product = lax.optimization_barrier(jnp.sum(query_wide * shifted(key_table, row_step, col_step), axis=-1)) * score_scale
        inside = (row_ids + row_step >= 0) & (row_ids + row_step < height) & (col_ids + col_step >= 0) & (col_ids + col_step < width) & (col_ids + col_step < valid)
        if row_step == 0 and col_step == 0:
            inside = jnp.ones_like(inside)
        score_list.append(jnp.where(inside[..., None], product, NEGATIVE))
    scores = jnp.stack(score_list)
    row_max = lax.optimization_barrier(jnp.max(scores, axis=0))
    log_total = row_max + jnp.log(lax.optimization_barrier(jnp.sum(jnp.exp(scores - row_max), axis=0)))
    weights = jnp.exp(scores - log_total)
    weights_low = lowered(weights)
    attended = jnp.zeros((height, width, head_count, HD), jnp.float32)
    for which, (row_step, col_step) in enumerate(offsets):
        attended = attended + weights_low[which][..., None] * shifted(value_table, row_step, col_step)
    row_dot = lax.optimization_barrier(jnp.sum(grad_table * attended, axis=-1))
    query_grad = jnp.zeros((height, width, head_count, HD), jnp.float32)
    key_grad = jnp.zeros(key_table.shape, jnp.float32)
    value_grad = jnp.zeros(value_table.shape, jnp.float32)
    for which, (row_step, col_step) in enumerate(offsets):
        key_part = shifted(key_table, row_step, col_step)
        value_part = shifted(value_table, row_step, col_step)
        weight_grad = lax.optimization_barrier(jnp.sum(grad_table * value_part, axis=-1))
        score_grad = lowered(weights[which] * (weight_grad - row_dot))
        query_grad = query_grad + score_grad[..., None] * key_part * score_scale
        row_lo = radius + row_step
        col_lo = radius + col_step
        key_grad = key_grad.at[row_lo:row_lo + height, col_lo:col_lo + width].add(score_grad[..., None] * query_wide * score_scale)
        value_grad = value_grad.at[row_lo:row_lo + height, col_lo:col_lo + width].add(weights_low[which][..., None] * grad_table)
    key_grad = key_grad[radius:radius + height, radius:radius + width].reshape(height, width, fine_width)
    value_grad = value_grad[radius:radius + height, radius:radius + width].reshape(height, width, fine_width)
    return (query_grad.reshape(height, width, fine_width).astype(jnp.bfloat16), jnp.concatenate([key_grad, value_grad], axis=-1).astype(jnp.bfloat16))

def reference(fine_q, fine_kv, coarse_q, coarse_kv, cotangent, gain_table, timesteps, valid_cols):
    frame_gain = gain_table[timesteps]
    scaled_grad = frame_gain[:, None, None, :] * cotangent.astype(jnp.float32)
    grad_fine_q, grad_fine_kv = lax.map(fine_frame, (fine_q, fine_kv, scaled_grad, valid_cols))
    half_pool = POOL // 2
    token_count = FRAMES * CROWS * CCOLS
    head_count = CWIDTH // HD
    score_scale = 1.0 / math.sqrt(HD)
    blocks = scaled_grad.reshape(FRAMES, CROWS, 2, half_pool, CCOLS, 2, half_pool, FWIDTH)
    pooled = lax.optimization_barrier(jnp.sum(blocks, axis=(3, 6))).transpose(0, 1, 3, 2, 4, 5).reshape(token_count, CWIDTH)
    coarse_grad = pooled.astype(jnp.bfloat16)
    token_ids = jnp.arange(token_count)
    frame_of = token_ids // (CROWS * CCOLS)
    col_of = token_ids % CCOLS
    key_ok = col_of * POOL < valid_cols[frame_of]

    def split(table):
        return table.reshape(token_count, head_count, HD).transpose(1, 0, 2)

    def coarse_head(record):
        query, keyset, valueset, grad = record
        scores = jnp.dot(query, keyset.T, preferred_element_type=jnp.float32) * score_scale
        scores = jnp.where(key_ok[None, :], scores, NEGATIVE)
        row_max = lax.optimization_barrier(jnp.max(scores, axis=-1, keepdims=True))
        log_total = row_max + jnp.log(lax.optimization_barrier(jnp.sum(jnp.exp(scores - row_max), axis=-1, keepdims=True)))
        weights = jnp.exp(scores - log_total)
        weights_low = weights.astype(jnp.bfloat16)
        attended = jnp.dot(weights_low, valueset, preferred_element_type=jnp.float32)
        row_dot = lax.optimization_barrier(jnp.sum(grad.astype(jnp.float32) * attended, axis=-1))
        weight_grad = jnp.dot(grad, valueset.T, preferred_element_type=jnp.float32)
        score_grad = (weights * (weight_grad - row_dot[:, None])).astype(jnp.bfloat16)
        query_grad = jnp.dot(score_grad, keyset, preferred_element_type=jnp.float32) * score_scale
        key_grad = jnp.dot(score_grad.T, query, preferred_element_type=jnp.float32) * score_scale
        value_grad = jnp.dot(weights_low.T, grad, preferred_element_type=jnp.float32)
        return (query_grad, key_grad, value_grad)
    query_all = split(coarse_q)
    key_all = split(coarse_kv[..., :CWIDTH])
    value_all = split(coarse_kv[..., CWIDTH:])
    grad_all = split(coarse_grad)
    query_grad, key_grad, value_grad = lax.map(coarse_head, (query_all, key_all, value_all, grad_all))

    def merge(table):
        return table.transpose(1, 0, 2).reshape(FRAMES, CROWS, CCOLS, CWIDTH).astype(jnp.bfloat16)
    return (grad_fine_q, grad_fine_kv, merge(query_grad), merge(key_grad), merge(value_grad))
```

```python
import functools

import jax
import jax.numpy as jnp
from jax import lax
from jax.experimental import pallas as pl
from jax.experimental.pallas import tpu as pltpu
from jax.sharding import PartitionSpec as P

F = 16
NZ = 32
ROWS = 64
HALO = 48
PIX = 128
KEYS = PIX + 2 * HALO
TOK = 2048
QT = 256
NEG = -1e30
BF = jnp.bfloat16
F32 = jnp.float32
MESH = pl.DeviceIdType.MESH


def tree():
    children = {0: [3, -3, 1, -1]}
    for k in (3, 6, 9, 12):
        children[k] = [k + 3, k - 1, k + 1]
        children[-k] = [-k - 3, -k + 1, -k - 1]
    children[15] = [16, 14]
    children[-15] = [-14]
    cost = {0: 0.0}
    todo = [0]
    while todo:
        d = todo.pop(0)
        for c in children.get(d, []):
            cost[c] = cost[d] + 0.88 + 0.75 * abs(c - d)
            todo.append(c)
    order = sorted((d for d in cost if d), key=lambda d: (cost[d], -d))
    return children, order


def dot(a, b, ca, cb):
    return lax.dot_general(a, b, (((ca,), (cb,)), ((), ())), preferred_element_type=F32)


def kernel(
    ts, vc, fq_h, fkv_h, cot_h, cq_h, ckv_h, gain_h,
    dfq_h, dfkv_h, dq_h, dk_h, dv_h,
    fq, kv, cot, cq, ckv, gain, stage, land, buf,
    gs, dkv, rim_out, rim_in, a_ref, b_ref, t_ref, ld,
    o_fq, o_fkv, o_q, o_k, o_v,
    in_sem, out_sem, halo_s, halo_r, rim_s, rim_r, a2a_s, a2a_r, self_sem,
    z_s, z_r, x_s, x_r,
):
    f = lax.axis_index("frames")
    r = lax.axis_index("rows")
    xl = r // NZ
    z = lax.rem(r, NZ)

    def zdev(d):
        return (f, xl * NZ + lax.rem(z + d + NZ, NZ))

    xdev = (f, (1 - xl) * NZ + z)
    above = (f, lax.rem(r + ROWS - 1, ROWS))
    below = (f, lax.rem(r + 1, ROWS))

    loads = [
        pltpu.make_async_copy(src, dst, in_sem.at[i])
        for i, (src, dst) in enumerate(
            (
                (cq_h, cq),
                (ckv_h, ckv),
                (gain_h, gain),
                (cot_h, cot),
                (fq_h, fq),
                (fkv_h, kv.at[pl.ds(HALO, PIX)]),
            )
        )
    ]
    for c in loads:
        c.start()

    barrier = pltpu.get_barrier_semaphore()
    peers = [(lax.rem(f + k, F), r) for k in range(1, F)]
    peers += [zdev(1), zdev(-1), zdev(3), zdev(-3), xdev, above, below]
    for peer in peers:
        pl.semaphore_signal(barrier, inc=1, device_id=peer, device_id_type=MESH)

    for c in loads[:4]:
        c.wait()

    gain_row = gain[pl.ds(ts[0], 1), :]
    rows = []
    for a in range(2):
        t = cot[pl.ds(64 * a, 16), :].astype(F32)
        for i in range(1, 4):
            t = t + cot[pl.ds(64 * a + 16 * i, 16), :].astype(F32)
        rows.append([jnp.sum(t[4 * m : 4 * m + 4], axis=0, keepdims=True) * gain_row for m in range(4)])
    pooled = jnp.concatenate(
        [
            jnp.concatenate([rows[0][2 * c], rows[0][2 * c + 1], rows[1][2 * c], rows[1][2 * c + 1]], axis=1)
            for c in range(2)
        ],
        axis=0,
    )
    half = lax.broadcasted_iota(jnp.int32, (2, 1024), 1) % 128 < 64
    kv_all = ckv[...].astype(F32)
    for part, (one, two) in enumerate(((cq[...].astype(F32), kv_all[:, :1024]), (kv_all[:, 1024:], pooled))):
        even = jnp.where(half, one, pltpu.roll(two, 64, 1)).astype(BF)
        odd = jnp.where(half, pltpu.roll(one, 1024 - 64, 1), two).astype(BF)
        for j in range(8):
            stage[2 * j, part] = even[:, 128 * j : 128 * j + 128]
            stage[2 * j + 1, part] = odd[:, 128 * j : 128 * j + 128]

    pl.semaphore_wait(barrier, len(peers))

    def a2a(k):
        there = lax.rem(f + k, F)
        return pltpu.make_async_remote_copy(
            src_ref=stage.at[there], dst_ref=land.at[:, f],
            send_sem=a2a_s.at[k - 1], recv_sem=a2a_r.at[k - 1],
            device_id=(there, r), device_id_type=MESH,
        )

    def a2a_in(k):
        here = lax.rem(f + F - k, F)
        return pltpu.make_async_remote_copy(
            src_ref=stage.at[here], dst_ref=land.at[:, here],
            send_sem=a2a_s.at[k - 1], recv_sem=a2a_r.at[k - 1],
            device_id=(here, r), device_id_type=MESH,
        )

    for k in range(1, F):
        a2a(k).start()
    own = pltpu.make_async_copy(stage.at[f], land.at[:, f], self_sem)
    own.start()

    halos = [
        pltpu.make_async_remote_copy(
            src_ref=fkv_h.at[pl.ds(PIX - HALO, HALO)], dst_ref=kv.at[pl.ds(0, HALO)],
            send_sem=halo_s.at[0], recv_sem=halo_r.at[0], device_id=below, device_id_type=MESH,
        ),
        pltpu.make_async_remote_copy(
            src_ref=fkv_h.at[pl.ds(0, HALO)], dst_ref=kv.at[pl.ds(HALO + PIX, HALO)],
            send_sem=halo_s.at[1], recv_sem=halo_r.at[1], device_id=above, device_id_type=MESH,
        ),
    ]
    for c in halos:
        c.start()

    own.wait()
    for k in range(1, F):
        a2a_in(k).wait_recv()
    for part in range(2):
        for i in range(F):
            buf[part, 0, 2 * i : 2 * i + 2, :] = land[part, i]

    children, order = tree()

    def pass_z(d, c):
        return pltpu.make_async_remote_copy(
            src_ref=buf.at[:, d % NZ], dst_ref=buf.at[:, c % NZ],
            send_sem=z_s.at[c % NZ], recv_sem=z_r.at[c % NZ],
            device_id=zdev(c - d), device_id_type=MESH,
        )

    def pass_x(d):
        return pltpu.make_async_remote_copy(
            src_ref=buf.at[:, d % NZ], dst_ref=buf.at[:, NZ + d % NZ],
            send_sem=x_s.at[d % NZ], recv_sem=x_r.at[d % NZ],
            device_id=xdev, device_id_type=MESH,
        )

    parent = {c: d for d, cs in children.items() for c in cs}

    def hand_on(d):
        for c in children.get(d, []):
            pass_z(d, c).start()
        pass_x(d).start()

    def arrive(d):
        pass_z(parent[d], d).wait_recv()
        hand_on(d)

    lane = lax.broadcasted_iota(jnp.int32, (PIX, 128), 1)

    def fine_prepare():
        for c in loads[4:]:
            c.wait()
        for c in halos:
            c.wait_recv()
        for p in range(2):
            cols = slice(128 * p, 128 * p + 128)
            q = fq[:, cols].astype(F32) * 0.125
            g = cot[:, cols].astype(F32) * gain_row[:, cols]
            for e in range(2):
                mine = lane < 64 if e == 0 else lane >= 64
                gs[0, p, pl.ds(PIX * e, PIX), :] = jnp.where(mine, q, 0.0).astype(BF)
                gs[1, p, pl.ds(PIX * e, PIX), :] = jnp.where(mine, g, 0.0).astype(BF)

    def fine_pair(p):
        qs = gs[0, p]
        g = gs[1, p]
        keys = kv[:, 128 * p : 128 * p + 128]
        values = kv[:, 256 + 128 * p : 256 + 128 * p + 128]
        qi = lax.broadcasted_iota(jnp.int32, (2 * PIX, KEYS), 0) % PIX
        ki = lax.broadcasted_iota(jnp.int32, (2 * PIX, KEYS), 1)
        dr = ki // 16 - 3 - qi // 16
        kc = ki % 16
        dc = kc - qi % 16
        row = r * 8 + ki // 16 - 3
        near = (jnp.abs(dr) <= 3) & (jnp.abs(dc) <= 3) & (row >= 0) & (row < ROWS * 8) & (kc < vc[f])
        near = near | ((dr == 0) & (dc == 0))
        s = jnp.where(near, dot(qs, keys, 1, 1), NEG)
        top = jnp.max(s, axis=1, keepdims=True)
        e = jnp.exp(s - top)
        w = e / jnp.sum(e, axis=1, keepdims=True)
        low = w.astype(BF)
        out = dot(low, values, 1, 0)
        row_dot = jnp.sum(g.astype(F32) * out, axis=1, keepdims=True)
        wg = dot(g, values, 1, 1)
        sg = (w * (wg - row_dot)).astype(BF)
        dq = dot(sg, keys, 1, 0) * 0.125
        o_fq[:, 128 * p : 128 * p + 128] = jnp.where(lane < 64, dq[:PIX], dq[PIX:]).astype(BF)
        dkv[:, 128 * p : 128 * p + 128] = dot(sg, qs, 0, 0)
        dkv[:, 256 + 128 * p : 256 + 128 * p + 128] = dot(low, g, 0, 0)

    rims = [
        pltpu.make_async_remote_copy(
            src_ref=rim_out.at[0], dst_ref=rim_in.at[0],
            send_sem=rim_s.at[0], recv_sem=rim_r.at[0], device_id=above, device_id_type=MESH,
        ),
        pltpu.make_async_remote_copy(
            src_ref=rim_out.at[1], dst_ref=rim_in.at[1],
            send_sem=rim_s.at[1], recv_sem=rim_r.at[1], device_id=below, device_id_type=MESH,
        ),
    ]
    fine_out = [
        pltpu.make_async_copy(o_fq, dfq_h, out_sem.at[0]),
        pltpu.make_async_copy(o_fkv, dfkv_h, out_sem.at[1]),
    ]

    def fine_send():
        rim_out[0] = dkv[pl.ds(0, HALO), :].astype(BF)
        rim_out[1] = dkv[pl.ds(HALO + PIX, HALO), :].astype(BF)
        for c in rims:
            c.start()
        fine_out[0].start()

    def fine_finish():
        for c in rims:
            c.wait_recv()
        mid = PIX - 2 * HALO
        o_fkv[pl.ds(0, HALO), :] = (dkv[pl.ds(HALO, HALO), :] + rim_in[1].astype(F32)).astype(BF)
        o_fkv[pl.ds(HALO, mid), :] = dkv[pl.ds(2 * HALO, mid), :].astype(BF)
        o_fkv[pl.ds(HALO + mid, HALO), :] = (
            dkv[pl.ds(2 * HALO + mid, HALO), :] + rim_in[0].astype(F32)
        ).astype(BF)
        fine_out[1].start()

    work = {1: [fine_prepare], 3: [functools.partial(fine_pair, 0)], -3: [],
            -4: [functools.partial(fine_pair, 1), fine_send], -10: [fine_finish]}

    hand_on(0)
    for d in order:
        arrive(d)
        for piece in work.get(d, []):
            piece()
    for d in [0] + order:
        pass_x(d).wait_recv()

    tl = lax.broadcasted_iota(jnp.int32, (32, 128), 1)
    ti = lax.broadcasted_iota(jnp.int32, (32, 128), 0)
    limit = jnp.zeros((32, 128), jnp.int32)
    for i in range(F):
        limit = jnp.where(ti // 2 == i, vc[i], limit)
    bias = jnp.where((tl == 0) & ((ti % 2) * 8 >= limit), NEG, 0.0).astype(F32)
    unit = jnp.where(tl == 0, 1.0, 0.0).astype(F32)
    bias3 = jnp.broadcast_to(bias[None], (8, 32, 128)).reshape(256, 128)
    unit3 = jnp.broadcast_to(unit[None], (8, 32, 128)).reshape(256, 128)
    upper = lax.broadcasted_iota(jnp.int32, (256, 128), 1) >= 64
    for i in range(8):
        at = pl.ds(256 * i, 256)
        qk = buf[0, 8 * i : 8 * i + 8].reshape(256, 128).astype(F32)
        a_ref[at, :] = jnp.where(upper, qk * 0.125, bias3).astype(BF)
        b_ref[at, :] = jnp.where(upper, pltpu.roll(qk, 64, 1), unit3).astype(BF)
        vg = buf[1, 8 * i : 8 * i + 8].reshape(256, 128).astype(F32)
        t_ref[:, 256 * i : 256 * i + 256] = jnp.transpose(vg, (1, 0)).astype(BF)

    def tile(i, carry):
        at = pl.multiple_of(i * QT, QT)
        s = dot(a_ref[...], b_ref[pl.ds(at, QT), :], 1, 1)
        top = jnp.max(s, axis=0, keepdims=True)
        e = jnp.exp(s - top)
        total = jnp.sum(e, axis=0, keepdims=True)
        out = dot(t_ref[pl.ds(0, 64), :], e.astype(BF), 1, 0)
        g = t_ref[pl.ds(64, 64), pl.ds(at, QT)].astype(F32)
        ld[0:1, pl.ds(at, QT)] = top + jnp.log(total)
        ld[1:2, pl.ds(at, QT)] = jnp.sum(g * out, axis=0, keepdims=True) / total
        return carry

    lax.fori_loop(0, TOK // QT, tile, 0)

    qk = buf[0].reshape(TOK, 128)
    vg = buf[1].reshape(TOK, 128)
    vt = t_ref[pl.ds(0, 64), :]
    gt = t_ref[pl.ds(64, 64), :]
    mine = buf[1, 0].astype(F32)
    v_own = mine[:, :64].astype(BF)
    g_wide = pltpu.roll(mine, 64, 1)[:, :64]
    g_own = g_wide.astype(BF)

    s = dot(a_ref[0:32, :], b_ref[...], 1, 1)
    w = jnp.exp(s - ld[0:1, :])
    dw = dot(v_own, gt, 1, 0)
    sg = (w * (dw - ld[1:2, :])).astype(BF)
    o_v[...] = dot(w.astype(BF), vg, 1, 0)[:, 64:].astype(BF)
    o_k[...] = (dot(sg, qk, 1, 0)[:, :64] * 0.125).astype(BF)

    s = dot(b_ref[0:32, :], a_ref[...], 1, 1)
    top = jnp.max(s, axis=1, keepdims=True)
    e = jnp.exp(s - top)
    w = e / jnp.sum(e, axis=1, keepdims=True)
    out = dot(w.astype(BF), vg, 1, 0)[:, :64]
    row_dot = jnp.sum(g_wide * out, axis=1, keepdims=True)
    dw = dot(g_own, vt, 1, 0)
    sg = (w * (dw - row_dot)).astype(BF)
    o_q[...] = (dot(sg, qk, 1, 0)[:, 64:] * 0.125).astype(BF)

    outs = [
        pltpu.make_async_copy(o_q, dq_h, out_sem.at[2]),
        pltpu.make_async_copy(o_k, dk_h, out_sem.at[3]),
        pltpu.make_async_copy(o_v, dv_h, out_sem.at[4]),
    ]
    for c in outs:
        c.start()
    for k in range(1, F):
        a2a(k).wait_send()
    for c in halos + rims:
        c.wait_send()
    for d in order:
        pass_z(parent[d], d).wait_send()
    for d in [0] + order:
        pass_x(d).wait_send()
    for c in fine_out + outs:
        c.wait()


def local(fine_q, fine_kv, coarse_q, coarse_kv, cotangent, gain_table, timesteps, valid_cols):
    smem = pl.BlockSpec(memory_space=pltpu.SMEM)
    hbm = pl.BlockSpec(memory_space=pl.ANY)
    vmem = pltpu.VMEM
    dma = pltpu.SemaphoreType.DMA
    dfq, dfkv, dq, dk, dv = pl.pallas_call(
        kernel,
        out_shape=(
            jax.ShapeDtypeStruct((PIX, 256), BF),
            jax.ShapeDtypeStruct((PIX, 512), BF),
            jax.ShapeDtypeStruct((32, 64), BF),
            jax.ShapeDtypeStruct((32, 64), BF),
            jax.ShapeDtypeStruct((32, 64), BF),
        ),
        in_specs=[smem, smem] + [hbm] * 6,
        out_specs=(hbm,) * 5,
        scratch_shapes=[
            vmem((PIX, 256), BF), vmem((KEYS, 512), BF), vmem((PIX, 256), BF),
            vmem((2, 1024), BF), vmem((2, 2048), BF), vmem((1000, 256), F32),
            vmem((F, 2, 2, 128), BF), vmem((2, F, 2, 128), BF), vmem((2, 2 * NZ, 32, 128), BF),
            vmem((2, 2, 2 * PIX, 128), BF), vmem((KEYS, 512), F32),
            vmem((2, HALO, 512), BF), vmem((2, HALO, 512), BF),
            vmem((TOK, 128), BF), vmem((TOK, 128), BF), vmem((128, TOK), BF), vmem((8, TOK), F32),
            vmem((PIX, 256), BF), vmem((PIX, 512), BF),
            vmem((32, 64), BF), vmem((32, 64), BF), vmem((32, 64), BF),
            dma((6,)), dma((5,)), dma((2,)), dma((2,)), dma((2,)), dma((2,)),
            dma((F - 1,)), dma((F - 1,)), dma,
            dma((NZ,)), dma((NZ,)), dma((NZ,)), dma((NZ,)),
        ],
        compiler_params=pltpu.CompilerParams(
            collective_id=0, has_side_effects=True, vmem_limit_bytes=48 * 1024 * 1024
        ),
    )(
        timesteps, valid_cols,
        fine_q.reshape(PIX, 256), fine_kv.reshape(PIX, 512), cotangent.reshape(PIX, 256),
        coarse_q.reshape(2, 1024), coarse_kv.reshape(2, 2048), gain_table,
    )
    return (
        dfq.reshape(1, 8, 16, 256), dfkv.reshape(1, 8, 16, 512),
        dq.reshape(F, 1, 2, 64), dk.reshape(F, 1, 2, 64), dv.reshape(F, 1, 2, 64),
    )


def solution(mesh):
    placed = P("frames", "rows", None, None)
    heads = P(None, "rows", None, "frames")
    return jax.shard_map(
        local,
        mesh=mesh,
        in_specs=(placed, placed, placed, placed, placed, P(), P("frames"), P()),
        out_specs=(placed, placed, heads, heads, heads),
        check_vma=False,
    )
```

```python
import functools

import jax
import jax.numpy as jnp
from jax import lax
from jax.experimental import pallas as pl
from jax.experimental.pallas import tpu as pltpu
from jax.sharding import PartitionSpec as P

F = 16
NZ = 32
ROWS = 64
HALO = 48
PIX = 128
KEYS = PIX + 2 * HALO
TOK = 2048
QT = 256
KT = 128
NEG = -1e30
BF = jnp.bfloat16
F32 = jnp.float32
MESH = pl.DeviceIdType.MESH


def tree():
    children = {0: [5, -5, 1, -1, 2, -2]}
    for k in (5, 10):
        children[k] = [k + 5, k - 1, k + 1, k - 2, k + 2]
        children[-k] = [-k - 5, -k + 1, -k - 1, -k + 2, -k - 2]
    children[15] = [16, 14, 13]
    children[-15] = [-14, -13]
    cost = {0: 0.0}
    todo = [0]
    while todo:
        d = todo.pop(0)
        for c in children.get(d, []):
            cost[c] = cost[d] + 2.0 + 0.6 * abs(c - d)
            todo.append(c)
    order = sorted((d for d in cost if d), key=lambda d: (cost[d], -d))
    return children, order


def dot(a, b, ca, cb):
    return lax.dot_general(a, b, (((ca,), (cb,)), ((), ())), preferred_element_type=F32)


def kernel(
    ts, vc, fq_h, fkv_h, cot_h, cq_h, ckv_h, gain_h,
    dfq_h, dfkv_h, dq_h, dk_h, dv_h,
    fq, kv, cot, cq, ckv, gain, stage, land, buf,
    gs, dkv, rim_out, rim_in, a_ref, b_ref, t_ref, g_ref, top_ref, sum_ref, dot_ref, bias_ref,
    o_fq, o_fkv, o_q, o_k, o_v,
    in_sem, out_sem, halo_s, halo_r, rim_s, rim_r, a2a_s, a2a_r, self_sem,
    z_s, z_r, x_s, x_r,
):
    f = lax.axis_index("frames")
    r = lax.axis_index("rows")
    xl = r // NZ
    z = lax.rem(r, NZ)

    def zdev(d):
        return (f, xl * NZ + lax.rem(z + d + NZ, NZ))

    xdev = (f, (1 - xl) * NZ + z)
    above = (f, lax.rem(r + ROWS - 1, ROWS))
    below = (f, lax.rem(r + 1, ROWS))

    children, order = tree()
    slots = {d: 2 * i for i, d in enumerate([0] + order)}

    loads = [
        pltpu.make_async_copy(src, dst, in_sem.at[i])
        for i, (src, dst) in enumerate(
            (
                (cq_h, cq),
                (ckv_h, ckv),
                (gain_h, gain),
                (cot_h, cot),
                (fq_h, fq),
                (fkv_h, kv.at[pl.ds(HALO, PIX)]),
            )
        )
    ]
    for c in loads:
        c.start()

    barrier = pltpu.get_barrier_semaphore()
    peers = [(lax.rem(f + k, F), r) for k in range(1, F)]
    peers += [zdev(1), zdev(-1), zdev(2), zdev(-2), zdev(5), zdev(-5), xdev, above, below]
    for peer in peers:
        pl.semaphore_signal(barrier, inc=1, device_id=peer, device_id_type=MESH)

    for c in loads[:4]:
        c.wait()

    gain_row = gain[pl.ds(ts[0], 1), :]
    rows = []
    for a in range(2):
        t = cot[pl.ds(64 * a, 16), :].astype(F32)
        for i in range(1, 4):
            t = t + cot[pl.ds(64 * a + 16 * i, 16), :].astype(F32)
        rows.append([jnp.sum(t[4 * m : 4 * m + 4], axis=0, keepdims=True) * gain_row for m in range(4)])
    pooled = jnp.concatenate(
        [
            jnp.concatenate([rows[0][2 * c], rows[0][2 * c + 1], rows[1][2 * c], rows[1][2 * c + 1]], axis=1)
            for c in range(2)
        ],
        axis=0,
    )
    half = lax.broadcasted_iota(jnp.int32, (2, 1024), 1) % 128 < 64
    kv_all = ckv[...].astype(F32)
    for part, (one, two) in enumerate(((cq[...].astype(F32), kv_all[:, :1024]), (kv_all[:, 1024:], pooled))):
        even = jnp.where(half, one, pltpu.roll(two, 64, 1)).astype(BF)
        odd = jnp.where(half, pltpu.roll(one, 1024 - 64, 1), two).astype(BF)
        for j in range(8):
            stage[2 * j, part] = even[:, 128 * j : 128 * j + 128]
            stage[2 * j + 1, part] = odd[:, 128 * j : 128 * j + 128]

    pl.semaphore_wait(barrier, len(peers))

    def a2a(k):
        there = lax.rem(f + k, F)
        return pltpu.make_async_remote_copy(
            src_ref=stage.at[there], dst_ref=land.at[:, f],
            send_sem=a2a_s.at[k - 1], recv_sem=a2a_r.at[k - 1],
            device_id=(there, r), device_id_type=MESH,
        )

    def a2a_in(k):
        here = lax.rem(f + F - k, F)
        return pltpu.make_async_remote_copy(
            src_ref=stage.at[here], dst_ref=land.at[:, here],
            send_sem=a2a_s.at[k - 1], recv_sem=a2a_r.at[k - 1],
            device_id=(here, r), device_id_type=MESH,
        )

    for k in range(1, F):
        a2a(k).start()
    own = pltpu.make_async_copy(stage.at[f], land.at[:, f], self_sem)
    own.start()

    halos = [
        pltpu.make_async_remote_copy(
            src_ref=fkv_h.at[pl.ds(PIX - HALO, HALO)], dst_ref=kv.at[pl.ds(0, HALO)],
            send_sem=halo_s.at[0], recv_sem=halo_r.at[0], device_id=below, device_id_type=MESH,
        ),
        pltpu.make_async_remote_copy(
            src_ref=fkv_h.at[pl.ds(0, HALO)], dst_ref=kv.at[pl.ds(HALO + PIX, HALO)],
            send_sem=halo_s.at[1], recv_sem=halo_r.at[1], device_id=above, device_id_type=MESH,
        ),
    ]
    for c in halos:
        c.start()

    own.wait()
    for k in range(1, F):
        a2a_in(k).wait_recv()
    for part in range(2):
        for i in range(F):
            buf[part, 0, 2 * i : 2 * i + 2, :] = land[part, i]


    def pass_z(d, c):
        return pltpu.make_async_remote_copy(
            src_ref=buf.at[:, slots[d]], dst_ref=buf.at[:, slots[c]],
            send_sem=z_s.at[c % NZ], recv_sem=z_r.at[c % NZ],
            device_id=zdev(c - d), device_id_type=MESH,
        )

    def pass_x(d):
        return pltpu.make_async_remote_copy(
            src_ref=buf.at[:, slots[d]], dst_ref=buf.at[:, slots[d] + 1],
            send_sem=x_s.at[d % NZ], recv_sem=x_r.at[d % NZ],
            device_id=xdev, device_id_type=MESH,
        )

    parent = {c: d for d, cs in children.items() for c in cs}

    def hand_on(d):
        for c in children.get(d, []):
            pass_z(d, c).start()
        pass_x(d).start()

    def arrive(d):
        pass_z(parent[d], d).wait_recv()
        hand_on(d)

    lane = lax.broadcasted_iota(jnp.int32, (PIX, 128), 1)

    def fine_prepare():
        for c in loads[4:]:
            c.wait()
        for c in halos:
            c.wait_recv()
        for p in range(2):
            cols = slice(128 * p, 128 * p + 128)
            q = fq[:, cols].astype(F32) * 0.125
            g = cot[:, cols].astype(F32) * gain_row[:, cols]
            for e in range(2):
                mine = lane < 64 if e == 0 else lane >= 64
                gs[0, p, pl.ds(PIX * e, PIX), :] = jnp.where(mine, q, 0.0).astype(BF)
                gs[1, p, pl.ds(PIX * e, PIX), :] = jnp.where(mine, g, 0.0).astype(BF)

    def fine_pair(p):
        qs = gs[0, p]
        g = gs[1, p]
        keys = kv[:, 128 * p : 128 * p + 128]
        values = kv[:, 256 + 128 * p : 256 + 128 * p + 128]
        qi = lax.broadcasted_iota(jnp.int32, (2 * PIX, KEYS), 0) % PIX
        ki = lax.broadcasted_iota(jnp.int32, (2 * PIX, KEYS), 1)
        dr = ki // 16 - 3 - qi // 16
        kc = ki % 16
        dc = kc - qi % 16
        row = r * 8 + ki // 16 - 3
        near = (jnp.abs(dr) <= 3) & (jnp.abs(dc) <= 3) & (row >= 0) & (row < ROWS * 8) & (kc < vc[f])
        near = near | ((dr == 0) & (dc == 0))
        s = jnp.where(near, dot(qs, keys, 1, 1), NEG)
        top = jnp.max(s, axis=1, keepdims=True)
        e = jnp.exp(s - top)
        w = e / jnp.sum(e, axis=1, keepdims=True)
        low = w.astype(BF)
        out = dot(low, values, 1, 0)
        row_dot = jnp.sum(g.astype(F32) * out, axis=1, keepdims=True)
        wg = dot(g, values, 1, 1)
        sg = (w * (wg - row_dot)).astype(BF)
        dq = dot(sg, keys, 1, 0) * 0.125
        o_fq[:, 128 * p : 128 * p + 128] = jnp.where(lane < 64, dq[:PIX], dq[PIX:]).astype(BF)
        dkv[:, 128 * p : 128 * p + 128] = dot(sg, qs, 0, 0)
        dkv[:, 256 + 128 * p : 256 + 128 * p + 128] = dot(low, g, 0, 0)

    rims = [
        pltpu.make_async_remote_copy(
            src_ref=rim_out.at[0], dst_ref=rim_in.at[0],
            send_sem=rim_s.at[0], recv_sem=rim_r.at[0], device_id=above, device_id_type=MESH,
        ),
        pltpu.make_async_remote_copy(
            src_ref=rim_out.at[1], dst_ref=rim_in.at[1],
            send_sem=rim_s.at[1], recv_sem=rim_r.at[1], device_id=below, device_id_type=MESH,
        ),
    ]
    fine_out = [
        pltpu.make_async_copy(o_fq, dfq_h, out_sem.at[0]),
        pltpu.make_async_copy(o_fkv, dfkv_h, out_sem.at[1]),
    ]

    def fine_send():
        rim_out[0] = dkv[pl.ds(0, HALO), :].astype(BF)
        rim_out[1] = dkv[pl.ds(HALO + PIX, HALO), :].astype(BF)
        for c in rims:
            c.start()
        fine_out[0].start()

    def fine_finish():
        for c in rims:
            c.wait_recv()
        mid = PIX - 2 * HALO
        o_fkv[pl.ds(0, HALO), :] = (dkv[pl.ds(HALO, HALO), :] + rim_in[1].astype(F32)).astype(BF)
        o_fkv[pl.ds(HALO, mid), :] = dkv[pl.ds(2 * HALO, mid), :].astype(BF)
        o_fkv[pl.ds(HALO + mid, HALO), :] = (
            dkv[pl.ds(2 * HALO + mid, HALO), :] + rim_in[0].astype(F32)
        ).astype(BF)
        fine_out[1].start()

    tl = lax.broadcasted_iota(jnp.int32, (32, 128), 1)
    ti = lax.broadcasted_iota(jnp.int32, (32, 128), 0)

    def coarse_prepare():
        limit = jnp.zeros((32, 128), jnp.int32)
        for i in range(F):
            limit = jnp.where(ti // 2 == i, vc[i], limit)
        bias = jnp.where((tl == 0) & ((ti % 2) * 8 >= limit), NEG, 0.0).astype(F32)
        bias_ref[...] = jnp.broadcast_to(bias[None], (8, 32, 128)).reshape(QT, 128)
        t_ref[pl.ds(64, 16), :] = jnp.ones((16, TOK), BF)

    def pair(q, c):
        qs, ks = pl.ds(QT * q, QT), pl.ds(KT * c, KT)
        s = dot(a_ref[ks, :], b_ref[qs, :], 1, 1)
        top = jnp.max(s, axis=0, keepdims=True)
        e = jnp.exp(s - top).astype(BF)
        out = dot(t_ref[:, ks], e, 1, 0)
        top_ref[c : c + 1, qs] = top
        sum_ref[c : c + 1, qs] = out[64:65]
        dot_ref[c : c + 1, qs] = jnp.sum(out[:64] * g_ref[:, qs], axis=0, keepdims=True)

    def coarse_tile(t):
        for d in ([0] + order)[4 * t : 4 * t + 4]:
            pass_x(d).wait_recv()
        at = pl.ds(QT * t, QT)
        upper = lax.broadcasted_iota(jnp.int32, (QT, 128), 1) >= 64
        unit = (lax.broadcasted_iota(jnp.int32, (QT, 128), 1) == 0).astype(F32)
        qk = buf[0, 8 * t : 8 * t + 8].reshape(QT, 128).astype(F32)
        a_ref[at, :] = jnp.where(upper, qk * 0.125, bias_ref[...]).astype(BF)
        b_ref[at, :] = jnp.where(upper, pltpu.roll(qk, 64, 1), unit).astype(BF)
        vg = jnp.transpose(buf[1, 8 * t : 8 * t + 8].reshape(QT, 128).astype(F32), (1, 0))
        t_ref[pl.ds(0, 64), at] = vg[:64].astype(BF)
        g_ref[:, at] = vg[64:]
        for i in range(t):
            pair(i, 2 * t)
            pair(i, 2 * t + 1)
        for c in range(2 * t + 2):
            pair(t, c)

    def tiles(*ts_):
        return [functools.partial(coarse_tile, t) for t in ts_]

    work = {
        2: [coarse_prepare],
        -5: [fine_prepare, functools.partial(fine_pair, 0), functools.partial(fine_pair, 1), fine_send],
        -10: tiles(0, 1, 2) + [fine_finish],
        -15: tiles(3, 4, 5),
    }

    hand_on(0)
    for d in order:
        arrive(d)
        for piece in work.get(d, []):
            piece()
    coarse_tile(6)
    coarse_tile(7)

    top = jnp.max(top_ref[...], axis=0, keepdims=True)
    share = jnp.exp(top_ref[...] - top)
    total = jnp.sum(share * sum_ref[...], axis=0, keepdims=True)
    log_total = top + jnp.log(total)
    dots = jnp.sum(share * dot_ref[...], axis=0, keepdims=True) / total

    qk = buf[0].reshape(TOK, 128)
    vg = buf[1].reshape(TOK, 128)
    mine = buf[1, 0].astype(F32)
    v_own = mine[:, :64].astype(BF)
    g_wide = pltpu.roll(mine, 64, 1)[:, :64]

    s = dot(a_ref[0:32, :], b_ref[...], 1, 1)
    w = jnp.exp(s - log_total)
    dw = dot(v_own, g_ref[...].astype(BF), 1, 0)
    sg = (w * (dw - dots)).astype(BF)
    o_v[...] = dot(w.astype(BF), vg, 1, 0)[:, 64:].astype(BF)
    o_k[...] = (dot(sg, qk, 1, 0)[:, :64] * 0.125).astype(BF)

    s = dot(b_ref[0:32, :], a_ref[...], 1, 1)
    top = jnp.max(s, axis=1, keepdims=True)
    e = jnp.exp(s - top)
    w = e / jnp.sum(e, axis=1, keepdims=True)
    out = dot(w.astype(BF), vg, 1, 0)[:, :64]
    row_dot = jnp.sum(g_wide * out, axis=1, keepdims=True)
    dw = dot(g_wide.astype(BF), t_ref[pl.ds(0, 64), :], 1, 0)
    sg = (w * (dw - row_dot)).astype(BF)
    o_q[...] = (dot(sg, qk, 1, 0)[:, 64:] * 0.125).astype(BF)

    outs = [
        pltpu.make_async_copy(o_q, dq_h, out_sem.at[2]),
        pltpu.make_async_copy(o_k, dk_h, out_sem.at[3]),
        pltpu.make_async_copy(o_v, dv_h, out_sem.at[4]),
    ]
    for c in outs:
        c.start()
    for k in range(1, F):
        a2a(k).wait_send()
    for c in halos + rims:
        c.wait_send()
    for d in order:
        pass_z(parent[d], d).wait_send()
    for d in [0] + order:
        pass_x(d).wait_send()
    for c in fine_out + outs:
        c.wait()


def placing(*refs):
    sem = refs[-1]
    copies = [pltpu.make_async_copy(refs[i], refs[5 + i], sem.at[i]) for i in range(5)]
    for c in copies:
        c.start()
    for c in copies:
        c.wait()


def local(fine_q, fine_kv, coarse_q, coarse_kv, cotangent, gain_table, timesteps, valid_cols):
    smem = pl.BlockSpec(memory_space=pltpu.SMEM)
    hbm = pl.BlockSpec(memory_space=pl.ANY)
    vmem = pltpu.VMEM
    dma = pltpu.SemaphoreType.DMA
    shapes = (
        jax.ShapeDtypeStruct((PIX, 256), BF),
        jax.ShapeDtypeStruct((PIX, 512), BF),
        jax.ShapeDtypeStruct((32, 64), BF),
        jax.ShapeDtypeStruct((32, 64), BF),
        jax.ShapeDtypeStruct((32, 64), BF),
    )
    made = pl.pallas_call(
        kernel,
        out_shape=shapes,
        in_specs=[smem, smem] + [pl.BlockSpec(memory_space=pltpu.HBM)] * 6,
        out_specs=(hbm,) * 5,
        scratch_shapes=[
            vmem((PIX, 256), BF), vmem((KEYS, 512), BF), vmem((PIX, 256), BF),
            vmem((2, 1024), BF), vmem((2, 2048), BF), vmem((1000, 256), F32),
            vmem((F, 2, 2, 128), BF), vmem((2, F, 2, 128), BF), vmem((2, 2 * NZ, 32, 128), BF),
            vmem((2, 2, 2 * PIX, 128), BF), vmem((KEYS, 512), F32),
            vmem((2, HALO, 512), BF), vmem((2, HALO, 512), BF),
            vmem((TOK, 128), BF), vmem((TOK, 128), BF), vmem((80, TOK), BF), vmem((64, TOK), F32),
            vmem((16, TOK), F32), vmem((16, TOK), F32), vmem((16, TOK), F32), vmem((QT, 128), F32),
            vmem((PIX, 256), BF), vmem((PIX, 512), BF),
            vmem((32, 64), BF), vmem((32, 64), BF), vmem((32, 64), BF),
            dma((6,)), dma((5,)), dma((2,)), dma((2,)), dma((2,)), dma((2,)),
            dma((F - 1,)), dma((F - 1,)), dma,
            dma((NZ,)), dma((NZ,)), dma((NZ,)), dma((NZ,)),
        ],
        compiler_params=pltpu.CompilerParams(
            collective_id=0, has_side_effects=True, vmem_limit_bytes=24 * 1024 * 1024
        ),
    )(
        timesteps, valid_cols,
        *(
            pltpu.with_memory_space_constraint(x, pltpu.HBM)
            for x in (
                fine_q.reshape(PIX, 256), fine_kv.reshape(PIX, 512), cotangent.reshape(PIX, 256),
                coarse_q.reshape(2, 1024), coarse_kv.reshape(2, 2048), gain_table,
            )
        ),
    )
    dfq, dfkv, dq, dk, dv = pl.pallas_call(
        placing,
        out_shape=shapes,
        in_specs=[hbm] * 5,
        out_specs=(pl.BlockSpec(memory_space=pltpu.HBM),) * 5,
        scratch_shapes=[dma((5,))],
        compiler_params=pltpu.CompilerParams(vmem_limit_bytes=1024 * 1024),
    )(*made)
    return (
        dfq.reshape(1, 8, 16, 256), dfkv.reshape(1, 8, 16, 512),
        dq.reshape(F, 1, 2, 64), dk.reshape(F, 1, 2, 64), dv.reshape(F, 1, 2, 64),
    )


def solution(mesh):
    placed = P("frames", "rows", None, None)
    heads = P(None, "rows", None, "frames")
    return jax.shard_map(
        local,
        mesh=mesh,
        in_specs=(placed, placed, placed, placed, placed, P(), P("frames"), P()),
        out_specs=(placed, placed, heads, heads, heads),
        check_vma=False,
    )
```

```python
import functools

import jax
import jax.numpy as jnp
from jax import lax
from jax.experimental import pallas as pl
from jax.experimental.pallas import tpu as pltpu
from jax.sharding import PartitionSpec as P

F = 16
NZ = 32
ROWS = 64
HALO = 48
PIX = 128
KEYS = PIX + 2 * HALO
TOK = 2048
QT = 256
KT = 128
NEG = -1e30
BF = jnp.bfloat16
F32 = jnp.float32
MESH = pl.DeviceIdType.MESH


def tree():
    children = {0: [5, -5, 1, -1, 2, -2]}
    for k in (5, 10):
        children[k] = [k + 5, k - 1, k + 1, k - 2, k + 2]
        children[-k] = [-k - 5, -k + 1, -k - 1, -k + 2, -k - 2]
    children[15] = [16, 14, 13]
    children[-15] = [-14, -13]
    cost = {0: 0.0}
    todo = [0]
    while todo:
        d = todo.pop(0)
        for c in children.get(d, []):
            cost[c] = cost[d] + 2.0 + 0.6 * abs(c - d)
            todo.append(c)
    order = sorted((d for d in cost if d), key=lambda d: (cost[d], -d))
    return children, order


def dot(a, b, ca, cb):
    return lax.dot_general(a, b, (((ca,), (cb,)), ((), ())), preferred_element_type=F32)


def kernel(
    ts, vc_h, fq_h, fkv_h, cot_h, cq_h, ckv_h, gain_h,
    dfq_h, dfkv_h, dq_h, dk_h, dv_h,
    vc, fq, kv, cot, cq, ckv, gain, stage, land, buf,
    gs, dkv, rim_out, rim_in, a_ref, b_ref, t_ref, g_ref, top_ref, sum_ref, dot_ref, bias_ref,
    o_fq, o_fkv, o_q, o_k, o_v,
    in_sem, out_sem, halo_s, halo_r, rim_s, rim_r, a2a_s, a2a_r, self_sem,
    z_s, z_r, x_s, x_r,
):
    f = lax.axis_index("frames")
    r = lax.axis_index("rows")
    xl = r // NZ
    z = lax.rem(r, NZ)

    def zdev(d):
        return (f, xl * NZ + lax.rem(z + d + NZ, NZ))

    xdev = (f, (1 - xl) * NZ + z)
    above = (f, lax.rem(r + ROWS - 1, ROWS))
    below = (f, lax.rem(r + 1, ROWS))

    children, order = tree()
    slots = {d: 2 * i for i, d in enumerate([0] + order)}

    loads = [
        pltpu.make_async_copy(src, dst, in_sem.at[i])
        for i, (src, dst) in enumerate(
            (
                (gain_h, gain),
                (cot_h, cot),
                (ckv_h, ckv),
                (cq_h, cq),
                (vc_h, vc),
                (fq_h, fq),
                (fkv_h, kv.at[pl.ds(HALO, PIX)]),
            )
        )
    ]
    barrier = pltpu.get_barrier_semaphore()
    peers = [(lax.rem(f + k, F), r) for k in range(1, F)]
    peers += [zdev(1), zdev(-1), zdev(2), zdev(-2), zdev(5), zdev(-5), xdev, above, below]
    for peer in peers:
        pl.semaphore_signal(barrier, inc=1, device_id=peer, device_id_type=MESH)

    for c in loads:
        c.start()

    for c in loads[:5]:
        c.wait()

    gain_row = gain[pl.ds(ts[0], 1), :]
    rows = []
    for a in range(2):
        t = cot[pl.ds(64 * a, 16), :].astype(F32)
        for i in range(1, 4):
            t = t + cot[pl.ds(64 * a + 16 * i, 16), :].astype(F32)
        rows.append([jnp.sum(t[4 * m : 4 * m + 4], axis=0, keepdims=True) * gain_row for m in range(4)])
    pooled = jnp.concatenate(
        [
            jnp.concatenate([rows[0][2 * c], rows[0][2 * c + 1], rows[1][2 * c], rows[1][2 * c + 1]], axis=1)
            for c in range(2)
        ],
        axis=0,
    )
    half = lax.broadcasted_iota(jnp.int32, (2, 1024), 1) % 128 < 64
    kv_all = ckv[...].astype(F32)
    for part, (one, two) in enumerate(((cq[...].astype(F32), kv_all[:, :1024]), (kv_all[:, 1024:], pooled))):
        even = jnp.where(half, one, pltpu.roll(two, 64, 1)).astype(BF)
        odd = jnp.where(half, pltpu.roll(one, 1024 - 64, 1), two).astype(BF)
        for j in range(8):
            stage[2 * j, part] = even[:, 128 * j : 128 * j + 128]
            stage[2 * j + 1, part] = odd[:, 128 * j : 128 * j + 128]

    pl.semaphore_wait(barrier, len(peers))

    def a2a(k):
        there = lax.rem(f + k, F)
        return pltpu.make_async_remote_copy(
            src_ref=stage.at[there], dst_ref=land.at[:, f],
            send_sem=a2a_s.at[k - 1], recv_sem=a2a_r.at[k - 1],
            device_id=(there, r), device_id_type=MESH,
        )

    def a2a_in(k):
        here = lax.rem(f + F - k, F)
        return pltpu.make_async_remote_copy(
            src_ref=stage.at[here], dst_ref=land.at[:, here],
            send_sem=a2a_s.at[k - 1], recv_sem=a2a_r.at[k - 1],
            device_id=(here, r), device_id_type=MESH,
        )

    for k in range(1, F):
        a2a(k).start()
    own = pltpu.make_async_copy(stage.at[f], land.at[:, f], self_sem)
    own.start()

    halos = [
        pltpu.make_async_remote_copy(
            src_ref=fkv_h.at[pl.ds(PIX - HALO, HALO)], dst_ref=kv.at[pl.ds(0, HALO)],
            send_sem=halo_s.at[0], recv_sem=halo_r.at[0], device_id=below, device_id_type=MESH,
        ),
        pltpu.make_async_remote_copy(
            src_ref=fkv_h.at[pl.ds(0, HALO)], dst_ref=kv.at[pl.ds(HALO + PIX, HALO)],
            send_sem=halo_s.at[1], recv_sem=halo_r.at[1], device_id=above, device_id_type=MESH,
        ),
    ]
    for c in halos:
        c.start()

    own.wait()
    for k in range(1, F):
        a2a_in(k).wait_recv()
    for part in range(2):
        for i in range(F):
            buf[part, 0, 2 * i : 2 * i + 2, :] = land[part, i]


    def pass_z(d, c):
        return pltpu.make_async_remote_copy(
            src_ref=buf.at[:, slots[d]], dst_ref=buf.at[:, slots[c]],
            send_sem=z_s.at[c % NZ], recv_sem=z_r.at[c % NZ],
            device_id=zdev(c - d), device_id_type=MESH,
        )

    def pass_x(d):
        return pltpu.make_async_remote_copy(
            src_ref=buf.at[:, slots[d]], dst_ref=buf.at[:, slots[d] + 1],
            send_sem=x_s.at[d % NZ], recv_sem=x_r.at[d % NZ],
            device_id=xdev, device_id_type=MESH,
        )

    parent = {c: d for d, cs in children.items() for c in cs}

    def hand_on(d):
        for c in children.get(d, []):
            pass_z(d, c).start()
        pass_x(d).start()

    def arrive(d):
        pass_z(parent[d], d).wait_recv()
        hand_on(d)

    lane = lax.broadcasted_iota(jnp.int32, (PIX, 128), 1)

    def fine_prepare():
        for c in loads[5:]:
            c.wait()
        for c in halos:
            c.wait_recv()
        for p in range(2):
            cols = slice(128 * p, 128 * p + 128)
            q = fq[:, cols].astype(F32) * 0.125
            g = cot[:, cols].astype(F32) * gain_row[:, cols]
            for e in range(2):
                mine = lane < 64 if e == 0 else lane >= 64
                gs[0, p, pl.ds(PIX * e, PIX), :] = jnp.where(mine, q, 0.0).astype(BF)
                gs[1, p, pl.ds(PIX * e, PIX), :] = jnp.where(mine, g, 0.0).astype(BF)

    def fine_pair(p):
        qs = gs[0, p]
        g = gs[1, p]
        keys = kv[:, 128 * p : 128 * p + 128]
        values = kv[:, 256 + 128 * p : 256 + 128 * p + 128]
        qi = lax.broadcasted_iota(jnp.int32, (2 * PIX, KEYS), 0) % PIX
        ki = lax.broadcasted_iota(jnp.int32, (2 * PIX, KEYS), 1)
        dr = ki // 16 - 3 - qi // 16
        kc = ki % 16
        dc = kc - qi % 16
        row = r * 8 + ki // 16 - 3
        near = (jnp.abs(dr) <= 3) & (jnp.abs(dc) <= 3) & (row >= 0) & (row < ROWS * 8) & (kc < vc[f])
        near = near | ((dr == 0) & (dc == 0))
        s = jnp.where(near, dot(qs, keys, 1, 1), NEG)
        top = jnp.max(s, axis=1, keepdims=True)
        e = jnp.exp(s - top)
        w = e / jnp.sum(e, axis=1, keepdims=True)
        low = w.astype(BF)
        out = dot(low, values, 1, 0)
        row_dot = jnp.sum(g.astype(F32) * out, axis=1, keepdims=True)
        wg = dot(g, values, 1, 1)
        sg = (w * (wg - row_dot)).astype(BF)
        dq = dot(sg, keys, 1, 0) * 0.125
        o_fq[:, 128 * p : 128 * p + 128] = jnp.where(lane < 64, dq[:PIX], dq[PIX:]).astype(BF)
        dkv[:, 128 * p : 128 * p + 128] = dot(sg, qs, 0, 0)
        dkv[:, 256 + 128 * p : 256 + 128 * p + 128] = dot(low, g, 0, 0)

    rims = [
        pltpu.make_async_remote_copy(
            src_ref=rim_out.at[0], dst_ref=rim_in.at[0],
            send_sem=rim_s.at[0], recv_sem=rim_r.at[0], device_id=above, device_id_type=MESH,
        ),
        pltpu.make_async_remote_copy(
            src_ref=rim_out.at[1], dst_ref=rim_in.at[1],
            send_sem=rim_s.at[1], recv_sem=rim_r.at[1], device_id=below, device_id_type=MESH,
        ),
    ]
    fine_out = [
        pltpu.make_async_copy(o_fq, dfq_h, out_sem.at[0]),
        pltpu.make_async_copy(o_fkv, dfkv_h, out_sem.at[1]),
    ]

    def fine_send():
        rim_out[0] = dkv[pl.ds(0, HALO), :].astype(BF)
        rim_out[1] = dkv[pl.ds(HALO + PIX, HALO), :].astype(BF)
        for c in rims:
            c.start()
        fine_out[0].start()

    def fine_finish():
        for c in rims:
            c.wait_recv()
        mid = PIX - 2 * HALO
        o_fkv[pl.ds(0, HALO), :] = (dkv[pl.ds(HALO, HALO), :] + rim_in[1].astype(F32)).astype(BF)
        o_fkv[pl.ds(HALO, mid), :] = dkv[pl.ds(2 * HALO, mid), :].astype(BF)
        o_fkv[pl.ds(HALO + mid, HALO), :] = (
            dkv[pl.ds(2 * HALO + mid, HALO), :] + rim_in[0].astype(F32)
        ).astype(BF)
        fine_out[1].start()

    tl = lax.broadcasted_iota(jnp.int32, (32, 128), 1)
    ti = lax.broadcasted_iota(jnp.int32, (32, 128), 0)

    def coarse_prepare():
        limit = jnp.zeros((32, 128), jnp.int32)
        for i in range(F):
            limit = jnp.where(ti // 2 == i, vc[i], limit)
        bias = jnp.where((tl == 0) & ((ti % 2) * 8 >= limit), NEG, 0.0).astype(F32)
        bias_ref[...] = jnp.broadcast_to(bias[None], (8, 32, 128)).reshape(QT, 128)
        t_ref[pl.ds(64, 16), :] = jnp.ones((16, TOK), BF)

    def score(q, c):
        return dot(a_ref[pl.ds(KT * c, KT), :], b_ref[pl.ds(QT * q, QT), :], 1, 1)

    def weigh(q, c, s):
        top = jnp.max(s, axis=0, keepdims=True)
        top_ref[c : c + 1, pl.ds(QT * q, QT)] = top
        return dot(t_ref[:, pl.ds(KT * c, KT)], jnp.exp(s - top).astype(BF), 1, 0)

    def settle(q, c, out):
        qs = pl.ds(QT * q, QT)
        sum_ref[c : c + 1, qs] = out[64:65]
        dot_ref[c : c + 1, qs] = jnp.sum(out[:64] * g_ref[:, qs], axis=0, keepdims=True)

    def parts(todo):
        depth = 8
        scores = [score(*p) for p in todo[:depth]]
        outs = []
        for i, p in enumerate(todo):
            if i + depth < len(todo):
                scores.append(score(*todo[i + depth]))
            outs.append(weigh(*p, scores[i]))
            if i >= depth:
                settle(*todo[i - depth], outs[i - depth])
        for i in range(max(0, len(todo) - depth), len(todo)):
            settle(*todo[i], outs[i])

    def coarse_tile(t):
        for d in ([0] + order)[4 * t : 4 * t + 4]:
            pass_x(d).wait_recv()
        at = pl.ds(QT * t, QT)
        upper = lax.broadcasted_iota(jnp.int32, (QT, 128), 1) >= 64
        unit = (lax.broadcasted_iota(jnp.int32, (QT, 128), 1) == 0).astype(F32)
        qk = buf[0, 8 * t : 8 * t + 8].reshape(QT, 128).astype(F32)
        a_ref[at, :] = jnp.where(upper, qk * 0.125, bias_ref[...]).astype(BF)
        b_ref[at, :] = jnp.where(upper, pltpu.roll(qk, 64, 1), unit).astype(BF)
        vg = jnp.transpose(buf[1, 8 * t : 8 * t + 8].reshape(QT, 128).astype(F32), (1, 0))
        t_ref[pl.ds(0, 64), at] = vg[:64].astype(BF)
        g_ref[:, at] = vg[64:]
        parts([(i, c) for i in range(t) for c in (2 * t, 2 * t + 1)] + [(t, c) for c in range(2 * t + 2)])

    def tiles(*ts_):
        return [functools.partial(coarse_tile, t) for t in ts_]

    work = {
        2: [coarse_prepare],
        -5: [fine_prepare, functools.partial(fine_pair, 0), functools.partial(fine_pair, 1), fine_send],
        -10: tiles(0, 1, 2) + [fine_finish],
        -15: tiles(3, 4, 5),
    }

    hand_on(0)
    for d in order:
        arrive(d)
        for piece in work.get(d, []):
            piece()
    coarse_tile(6)
    coarse_tile(7)

    top = jnp.max(top_ref[...], axis=0, keepdims=True)
    share = jnp.exp(top_ref[...] - top)
    total = jnp.sum(share * sum_ref[...], axis=0, keepdims=True)
    log_total = top + jnp.log(total)
    dots = jnp.sum(share * dot_ref[...], axis=0, keepdims=True) / total

    qk = buf[0].reshape(TOK, 128)
    vg = buf[1].reshape(TOK, 128)
    mine = buf[1, 0].astype(F32)
    v_own = mine[:, :64].astype(BF)
    g_wide = pltpu.roll(mine, 64, 1)[:, :64]

    s = dot(a_ref[0:32, :], b_ref[...], 1, 1)
    w = jnp.exp(s - log_total)
    dw = dot(v_own, g_ref[...].astype(BF), 1, 0)
    sg = (w * (dw - dots)).astype(BF)
    o_v[...] = dot(w.astype(BF), vg, 1, 0)[:, 64:].astype(BF)
    o_k[...] = (dot(sg, qk, 1, 0)[:, :64] * 0.125).astype(BF)

    s = dot(b_ref[0:32, :], a_ref[...], 1, 1)
    top = jnp.max(s, axis=1, keepdims=True)
    e = jnp.exp(s - top)
    w = e / jnp.sum(e, axis=1, keepdims=True)
    out = dot(w.astype(BF), vg, 1, 0)[:, :64]
    row_dot = jnp.sum(g_wide * out, axis=1, keepdims=True)
    dw = dot(g_wide.astype(BF), t_ref[pl.ds(0, 64), :], 1, 0)
    sg = (w * (dw - row_dot)).astype(BF)
    o_q[...] = (dot(sg, qk, 1, 0)[:, 64:] * 0.125).astype(BF)

    outs = [
        pltpu.make_async_copy(o_q, dq_h, out_sem.at[2]),
        pltpu.make_async_copy(o_k, dk_h, out_sem.at[3]),
        pltpu.make_async_copy(o_v, dv_h, out_sem.at[4]),
    ]
    for c in outs:
        c.start()
    for k in range(1, F):
        a2a(k).wait_send()
    for c in halos + rims:
        c.wait_send()
    for d in order:
        pass_z(parent[d], d).wait_send()
    for d in [0] + order:
        pass_x(d).wait_send()
    for c in fine_out + outs:
        c.wait()


def placing(*refs):
    sem = refs[-1]
    copies = [pltpu.make_async_copy(refs[i], refs[5 + i], sem.at[i]) for i in range(5)]
    for c in copies:
        c.start()
    for c in copies:
        c.wait()


def local(fine_q, fine_kv, coarse_q, coarse_kv, cotangent, gain_table, timesteps, valid_cols):
    smem = pl.BlockSpec(memory_space=pltpu.SMEM)
    hbm = pl.BlockSpec(memory_space=pl.ANY)
    vmem = pltpu.VMEM
    dma = pltpu.SemaphoreType.DMA
    shapes = (
        jax.ShapeDtypeStruct((PIX, 256), BF),
        jax.ShapeDtypeStruct((PIX, 512), BF),
        jax.ShapeDtypeStruct((32, 64), BF),
        jax.ShapeDtypeStruct((32, 64), BF),
        jax.ShapeDtypeStruct((32, 64), BF),
    )
    made = pl.pallas_call(
        kernel,
        out_shape=shapes,
        in_specs=[smem] + [pl.BlockSpec(memory_space=pltpu.HBM)] * 7,
        out_specs=(hbm,) * 5,
        scratch_shapes=[
            pltpu.SMEM((F,), jnp.int32),
            vmem((PIX, 256), BF), vmem((KEYS, 512), BF), vmem((PIX, 256), BF),
            vmem((2, 1024), BF), vmem((2, 2048), BF), vmem((1000, 256), F32),
            vmem((F, 2, 2, 128), BF), vmem((2, F, 2, 128), BF), vmem((2, 2 * NZ, 32, 128), BF),
            vmem((2, 2, 2 * PIX, 128), BF), vmem((KEYS, 512), F32),
            vmem((2, HALO, 512), BF), vmem((2, HALO, 512), BF),
            vmem((TOK, 128), BF), vmem((TOK, 128), BF), vmem((80, TOK), BF), vmem((64, TOK), F32),
            vmem((16, TOK), F32), vmem((16, TOK), F32), vmem((16, TOK), F32), vmem((QT, 128), F32),
            vmem((PIX, 256), BF), vmem((PIX, 512), BF),
            vmem((32, 64), BF), vmem((32, 64), BF), vmem((32, 64), BF),
            dma((7,)), dma((5,)), dma((2,)), dma((2,)), dma((2,)), dma((2,)),
            dma((F - 1,)), dma((F - 1,)), dma,
            dma((NZ,)), dma((NZ,)), dma((NZ,)), dma((NZ,)),
        ],
        compiler_params=pltpu.CompilerParams(
            collective_id=0, has_side_effects=True, vmem_limit_bytes=24 * 1024 * 1024
        ),
    )(
        timesteps,
        *(
            pltpu.with_memory_space_constraint(x, pltpu.HBM)
            for x in (
                valid_cols,
                fine_q.reshape(PIX, 256), fine_kv.reshape(PIX, 512), cotangent.reshape(PIX, 256),
                coarse_q.reshape(2, 1024), coarse_kv.reshape(2, 2048), gain_table,
            )
        ),
    )
    dfq, dfkv, dq, dk, dv = pl.pallas_call(
        placing,
        out_shape=shapes,
        in_specs=[hbm] * 5,
        out_specs=(pl.BlockSpec(memory_space=pltpu.HBM),) * 5,
        scratch_shapes=[dma((5,))],
        compiler_params=pltpu.CompilerParams(vmem_limit_bytes=1024 * 1024),
    )(*made)
    return (
        dfq.reshape(1, 8, 16, 256), dfkv.reshape(1, 8, 16, 512),
        dq.reshape(F, 1, 2, 64), dk.reshape(F, 1, 2, 64), dv.reshape(F, 1, 2, 64),
    )


def solution(mesh):
    placed = P("frames", "rows", None, None)
    heads = P(None, "rows", None, "frames")
    return jax.shard_map(
        local,
        mesh=mesh,
        in_specs=(placed, placed, placed, placed, placed, P(), P("frames"), P()),
        out_specs=(placed, placed, heads, heads, heads),
        check_vma=False,
    )
```

```python
import functools

import jax
import jax.numpy as jnp
from jax import lax
from jax.experimental import pallas as pl
from jax.experimental.pallas import tpu as pltpu
from jax.sharding import PartitionSpec as P

F = 16
NZ = 32
ROWS = 64
HALO = 48
PIX = 128
KEYS = PIX + 2 * HALO
TOK = 2048
QT = 256
KT = 128
NEG = -1e30
BF = jnp.bfloat16
F32 = jnp.float32
MESH = pl.DeviceIdType.MESH


ROOTS = (0,)
SHARED = (16, 14, -14)


def tree():
    children = {0: [5, -5, 1, -1, 2, -2], 15: [16, 14], -15: [-14]}
    for k in (5, -5, 10, -10):
        sign = 1 if k > 0 else -1
        hops = (5, -1, 1, -2, 2, 3) if abs(k) == 10 else (5, -1, 1, -2, 2)
        children[k] = [k + sign * h for h in hops]
    cost = {d: 4.4 + 0.6 * abs(d) for d in ROOTS}
    todo = list(ROOTS)
    while todo:
        d = todo.pop(0)
        for c in children.get(d, []):
            cost[c] = cost[d] + 2.0 + 0.6 * abs(c - d)
            todo.append(c)
    order = sorted((d for d in cost if d), key=lambda d: (cost[d], -d))
    return children, order


def dot(a, b, ca, cb):
    return lax.dot_general(a, b, (((ca,), (cb,)), ((), ())), preferred_element_type=F32)


def kernel(
    ts, vc_h, fq_h, fkv_h, cot_h, cq_h, ckv_h, gain_h,
    dfq_h, dfkv_h, dq_h, dk_h, dv_h,
    vc, fq, kv, cot, cq, ckv, gain, stage, land, buf,
    gs, dkv, rim_out, rim_in, a_ref, b_ref, t_ref, g_ref, top_ref, sum_ref, dot_ref, bias_ref,
    o_fq, o_fkv, o_q, o_k, o_v,
    in_sem, out_sem, halo_s, halo_r, rim_s, rim_r, a2a_s, a2a_r, self_sem,
    z_s, z_r, x_s, x_r,
):
    f = lax.axis_index("frames")
    r = lax.axis_index("rows")
    xl = r // NZ
    z = lax.rem(r, NZ)

    def zdev(d, head=f, column=xl):
        return (head, column * NZ + lax.rem(z + d + NZ, NZ))

    xdev = (f, (1 - xl) * NZ + z)
    above = (f, lax.rem(r + ROWS - 1, ROWS))
    below = (f, lax.rem(r + 1, ROWS))

    children, order = tree()
    slots = {d: 2 * i for i, d in enumerate([0] + order)}
    parent = {c: d for d, cs in children.items() for c in cs}

    loads = [
        pltpu.make_async_copy(src, dst, in_sem.at[i])
        for i, (src, dst) in enumerate(
            (
                (gain_h, gain),
                (cot_h, cot),
                (ckv_h, ckv),
                (cq_h, cq),
                (vc_h, vc),
                (fq_h, fq),
                (fkv_h, kv.at[pl.ds(HALO, PIX)]),
            )
        )
    ]
    barrier = pltpu.get_barrier_semaphore()
    hops = sorted({c - d for d, cs in children.items() for c in cs} | {d - c for d, cs in children.items() for c in cs})
    skew = sorted({s * (c - parent[c]) for c in SHARED for s in (1, -1)})
    peers = [zdev(o, lax.rem(f + k, F)) for o in ROOTS for k in range(F) if o or k]
    peers += [zdev(o) for o in hops] + [zdev(o, f, 1 - xl) for o in skew] + [xdev, above, below]
    for peer in peers:
        pl.semaphore_signal(barrier, inc=1, device_id=peer, device_id_type=MESH)

    for c in loads:
        c.start()

    for c in loads[:5]:
        c.wait()

    gain_row = gain[pl.ds(ts[0], 1), :]
    rows = []
    for a in range(2):
        t = cot[pl.ds(64 * a, 16), :].astype(F32)
        for i in range(1, 4):
            t = t + cot[pl.ds(64 * a + 16 * i, 16), :].astype(F32)
        rows.append([jnp.sum(t[4 * m : 4 * m + 4], axis=0, keepdims=True) * gain_row for m in range(4)])
    pooled = jnp.concatenate(
        [
            jnp.concatenate([rows[0][2 * c], rows[0][2 * c + 1], rows[1][2 * c], rows[1][2 * c + 1]], axis=1)
            for c in range(2)
        ],
        axis=0,
    )
    half = lax.broadcasted_iota(jnp.int32, (2, 1024), 1) % 128 < 64
    kv_all = ckv[...].astype(F32)
    for part, (one, two) in enumerate(((cq[...].astype(F32), kv_all[:, :1024]), (kv_all[:, 1024:], pooled))):
        even = jnp.where(half, one, pltpu.roll(two, 64, 1)).astype(BF)
        odd = jnp.where(half, pltpu.roll(one, 1024 - 64, 1), two).astype(BF)
        for j in range(8):
            stage[2 * j, part] = even[:, 128 * j : 128 * j + 128]
            stage[2 * j + 1, part] = odd[:, 128 * j : 128 * j + 128]

    pl.semaphore_wait(barrier, len(peers))

    def a2a(o, k):
        there = lax.rem(f + k, F)
        at = ROOTS.index(o)
        return pltpu.make_async_remote_copy(
            src_ref=stage.at[there], dst_ref=land.at[at, :, f],
            send_sem=a2a_s.at[at, k], recv_sem=a2a_r.at[at, k],
            device_id=zdev(o, there), device_id_type=MESH,
        )

    def a2a_in(o, k):
        here = lax.rem(f + F - k, F)
        at = ROOTS.index(o)
        return pltpu.make_async_remote_copy(
            src_ref=stage.at[here], dst_ref=land.at[at, :, here],
            send_sem=a2a_s.at[at, k], recv_sem=a2a_r.at[at, k],
            device_id=zdev(-o, here), device_id_type=MESH,
        )

    sends = [(o, k) for o in ROOTS for k in range(F) if o or k]
    own = pltpu.make_async_copy(stage.at[f], land.at[ROOTS.index(0), :, f], self_sem)
    own.start()
    for o, k in sends:
        a2a(o, k).start()

    halos = [
        pltpu.make_async_remote_copy(
            src_ref=fkv_h.at[pl.ds(PIX - HALO, HALO)], dst_ref=kv.at[pl.ds(0, HALO)],
            send_sem=halo_s.at[0], recv_sem=halo_r.at[0], device_id=below, device_id_type=MESH,
        ),
        pltpu.make_async_remote_copy(
            src_ref=fkv_h.at[pl.ds(0, HALO)], dst_ref=kv.at[pl.ds(HALO + PIX, HALO)],
            send_sem=halo_s.at[1], recv_sem=halo_r.at[1], device_id=above, device_id_type=MESH,
        ),
    ]
    for c in halos:
        c.start()

    def gather_heads(o):
        if o == 0:
            own.wait()
        for k in range(F):
            if o or k:
                a2a_in(o, k).wait_recv()
        for part in range(2):
            for i in range(F):
                buf[part, slots[o], 2 * i : 2 * i + 2, :] = land[ROOTS.index(o), part, i]

    def pass_z(d, c):
        return pltpu.make_async_remote_copy(
            src_ref=buf.at[:, slots[d]], dst_ref=buf.at[:, slots[c]],
            send_sem=z_s.at[c % NZ], recv_sem=z_r.at[c % NZ],
            device_id=zdev(c - d), device_id_type=MESH,
        )

    def pass_x(d):
        return pltpu.make_async_remote_copy(
            src_ref=buf.at[:, slots[d]], dst_ref=buf.at[:, slots[d] + 1],
            send_sem=x_s.at[d % NZ], recv_sem=x_r.at[d % NZ],
            device_id=xdev, device_id_type=MESH,
        )

    def pass_both(c):
        d = parent[c]
        return pltpu.make_async_remote_copy(
            src_ref=buf.at[:, slots[d]], dst_ref=buf.at[:, slots[c] + 1],
            send_sem=x_s.at[c % NZ], recv_sem=x_r.at[c % NZ],
            device_id=zdev(c - d, f, 1 - xl), device_id_type=MESH,
        )

    def other(d):
        return pass_both(d) if d in SHARED else pass_x(d)

    def hand_on(d):
        for c in children.get(d, []):
            pass_z(d, c).start()
            if c in SHARED:
                pass_both(c).start()
        if d not in SHARED:
            pass_x(d).start()

    def arrive(d):
        if d in ROOTS:
            gather_heads(d)
        else:
            pass_z(parent[d], d).wait_recv()
        hand_on(d)

    lane = lax.broadcasted_iota(jnp.int32, (PIX, 128), 1)

    def fine_prepare():
        for c in loads[5:]:
            c.wait()
        for c in halos:
            c.wait_recv()
        for p in range(2):
            cols = slice(128 * p, 128 * p + 128)
            q = fq[:, cols].astype(F32) * 0.125
            g = cot[:, cols].astype(F32) * gain_row[:, cols]
            for e in range(2):
                mine = lane < 64 if e == 0 else lane >= 64
                gs[0, p, pl.ds(PIX * e, PIX), :] = jnp.where(mine, q, 0.0).astype(BF)
                gs[1, p, pl.ds(PIX * e, PIX), :] = jnp.where(mine, g, 0.0).astype(BF)

    def fine_pair(p):
        qs = gs[0, p]
        g = gs[1, p]
        keys = kv[:, 128 * p : 128 * p + 128]
        values = kv[:, 256 + 128 * p : 256 + 128 * p + 128]
        qi = lax.broadcasted_iota(jnp.int32, (2 * PIX, KEYS), 0) % PIX
        ki = lax.broadcasted_iota(jnp.int32, (2 * PIX, KEYS), 1)
        dr = ki // 16 - 3 - qi // 16
        kc = ki % 16
        dc = kc - qi % 16
        row = r * 8 + ki // 16 - 3
        near = (jnp.abs(dr) <= 3) & (jnp.abs(dc) <= 3) & (row >= 0) & (row < ROWS * 8) & (kc < vc[f])
        near = near | ((dr == 0) & (dc == 0))
        s = jnp.where(near, dot(qs, keys, 1, 1), NEG)
        top = jnp.max(s, axis=1, keepdims=True)
        e = jnp.exp(s - top)
        w = e / jnp.sum(e, axis=1, keepdims=True)
        low = w.astype(BF)
        out = dot(low, values, 1, 0)
        row_dot = jnp.sum(g.astype(F32) * out, axis=1, keepdims=True)
        wg = dot(g, values, 1, 1)
        sg = (w * (wg - row_dot)).astype(BF)
        dq = dot(sg, keys, 1, 0) * 0.125
        o_fq[:, 128 * p : 128 * p + 128] = jnp.where(lane < 64, dq[:PIX], dq[PIX:]).astype(BF)
        dkv[:, 128 * p : 128 * p + 128] = dot(sg, qs, 0, 0)
        dkv[:, 256 + 128 * p : 256 + 128 * p + 128] = dot(low, g, 0, 0)

    rims = [
        pltpu.make_async_remote_copy(
            src_ref=rim_out.at[0], dst_ref=rim_in.at[0],
            send_sem=rim_s.at[0], recv_sem=rim_r.at[0], device_id=above, device_id_type=MESH,
        ),
        pltpu.make_async_remote_copy(
            src_ref=rim_out.at[1], dst_ref=rim_in.at[1],
            send_sem=rim_s.at[1], recv_sem=rim_r.at[1], device_id=below, device_id_type=MESH,
        ),
    ]
    fine_out = [
        pltpu.make_async_copy(o_fq, dfq_h, out_sem.at[0]),
        pltpu.make_async_copy(o_fkv, dfkv_h, out_sem.at[1]),
    ]

    def fine_send():
        rim_out[0] = dkv[pl.ds(0, HALO), :].astype(BF)
        rim_out[1] = dkv[pl.ds(HALO + PIX, HALO), :].astype(BF)
        for c in rims:
            c.start()
        fine_out[0].start()

    def fine_finish():
        for c in rims:
            c.wait_recv()
        mid = PIX - 2 * HALO
        o_fkv[pl.ds(0, HALO), :] = (dkv[pl.ds(HALO, HALO), :] + rim_in[1].astype(F32)).astype(BF)
        o_fkv[pl.ds(HALO, mid), :] = dkv[pl.ds(2 * HALO, mid), :].astype(BF)
        o_fkv[pl.ds(HALO + mid, HALO), :] = (
            dkv[pl.ds(2 * HALO + mid, HALO), :] + rim_in[0].astype(F32)
        ).astype(BF)
        fine_out[1].start()

    tl = lax.broadcasted_iota(jnp.int32, (32, 128), 1)
    ti = lax.broadcasted_iota(jnp.int32, (32, 128), 0)

    def coarse_prepare():
        limit = jnp.zeros((32, 128), jnp.int32)
        for i in range(F):
            limit = jnp.where(ti // 2 == i, vc[i], limit)
        bias = jnp.where((tl == 0) & ((ti % 2) * 8 >= limit), NEG, 0.0).astype(F32)
        bias_ref[...] = jnp.broadcast_to(bias[None], (8, 32, 128)).reshape(QT, 128)
        t_ref[pl.ds(64, 16), :] = jnp.ones((16, TOK), BF)

    def score(q, c):
        return dot(a_ref[pl.ds(KT * c, KT), :], b_ref[pl.ds(QT * q, QT), :], 1, 1)

    def weigh(q, c, s):
        top = jnp.max(s, axis=0, keepdims=True)
        top_ref[c : c + 1, pl.ds(QT * q, QT)] = top
        return dot(t_ref[:, pl.ds(KT * c, KT)], jnp.exp(s - top).astype(BF), 1, 0)

    def settle(q, c, out):
        qs = pl.ds(QT * q, QT)
        sum_ref[c : c + 1, qs] = out[64:65]
        dot_ref[c : c + 1, qs] = jnp.sum(out[:64] * g_ref[:, qs], axis=0, keepdims=True)

    def parts(todo):
        depth = 8
        scores = [score(*p) for p in todo[:depth]]
        outs = []
        for i, p in enumerate(todo):
            if i + depth < len(todo):
                scores.append(score(*todo[i + depth]))
            outs.append(weigh(*p, scores[i]))
            if i >= depth:
                settle(*todo[i - depth], outs[i - depth])
        for i in range(max(0, len(todo) - depth), len(todo)):
            settle(*todo[i], outs[i])

    def coarse_tile(t):
        for d in ([0] + order)[4 * t : 4 * t + 4]:
            other(d).wait_recv()
        at = pl.ds(QT * t, QT)
        upper = lax.broadcasted_iota(jnp.int32, (QT, 128), 1) >= 64
        unit = (lax.broadcasted_iota(jnp.int32, (QT, 128), 1) == 0).astype(F32)
        qk = buf[0, 8 * t : 8 * t + 8].reshape(QT, 128).astype(F32)
        a_ref[at, :] = jnp.where(upper, qk * 0.125, bias_ref[...]).astype(BF)
        b_ref[at, :] = jnp.where(upper, pltpu.roll(qk, 64, 1), unit).astype(BF)
        vg = jnp.transpose(buf[1, 8 * t : 8 * t + 8].reshape(QT, 128).astype(F32), (1, 0))
        t_ref[pl.ds(0, 64), at] = vg[:64].astype(BF)
        g_ref[:, at] = vg[64:]
        parts([(i, c) for i in range(t) for c in (2 * t, 2 * t + 1)] + [(t, c) for c in range(2 * t + 2)])

    def tiles(*ts_):
        return [functools.partial(coarse_tile, t) for t in ts_]

    work = {
        2: [coarse_prepare],
        -5: [fine_prepare, functools.partial(fine_pair, 0), functools.partial(fine_pair, 1), fine_send],
        -10: tiles(0, 1, 2) + [fine_finish],
        -15: tiles(3, 4, 5),
    }

    for d in [0] + order:
        arrive(d)
        for piece in work.get(d, []):
            piece()
    coarse_tile(6)
    coarse_tile(7)

    top = jnp.max(top_ref[...], axis=0, keepdims=True)
    share = jnp.exp(top_ref[...] - top)
    total = jnp.sum(share * sum_ref[...], axis=0, keepdims=True)
    log_total = top + jnp.log(total)
    dots = jnp.sum(share * dot_ref[...], axis=0, keepdims=True) / total

    qk = buf[0].reshape(TOK, 128)
    vg = buf[1].reshape(TOK, 128)
    mine = buf[1, 0].astype(F32)
    v_own = mine[:, :64].astype(BF)
    g_wide = pltpu.roll(mine, 64, 1)[:, :64]

    s = dot(a_ref[0:32, :], b_ref[...], 1, 1)
    w = jnp.exp(s - log_total)
    dw = dot(v_own, g_ref[...].astype(BF), 1, 0)
    sg = (w * (dw - dots)).astype(BF)
    o_v[...] = dot(w.astype(BF), vg, 1, 0)[:, 64:].astype(BF)
    o_k[...] = (dot(sg, qk, 1, 0)[:, :64] * 0.125).astype(BF)

    s = dot(b_ref[0:32, :], a_ref[...], 1, 1)
    top = jnp.max(s, axis=1, keepdims=True)
    e = jnp.exp(s - top)
    w = e / jnp.sum(e, axis=1, keepdims=True)
    out = dot(w.astype(BF), vg, 1, 0)[:, :64]
    row_dot = jnp.sum(g_wide * out, axis=1, keepdims=True)
    dw = dot(g_wide.astype(BF), t_ref[pl.ds(0, 64), :], 1, 0)
    sg = (w * (dw - row_dot)).astype(BF)
    o_q[...] = (dot(sg, qk, 1, 0)[:, 64:] * 0.125).astype(BF)

    outs = [
        pltpu.make_async_copy(o_q, dq_h, out_sem.at[2]),
        pltpu.make_async_copy(o_k, dk_h, out_sem.at[3]),
        pltpu.make_async_copy(o_v, dv_h, out_sem.at[4]),
    ]
    for c in outs:
        c.start()
    for o, k in sends:
        a2a(o, k).wait_send()
    for c in halos + rims:
        c.wait_send()
    for d in [0] + order:
        if d not in ROOTS:
            pass_z(parent[d], d).wait_send()
        other(d).wait_send()
    for c in fine_out + outs:
        c.wait()


def placing(*refs):
    sem = refs[-1]
    copies = [pltpu.make_async_copy(refs[i], refs[5 + i], sem.at[i]) for i in range(5)]
    for c in copies:
        c.start()
    for c in copies:
        c.wait()


def local(fine_q, fine_kv, coarse_q, coarse_kv, cotangent, gain_table, timesteps, valid_cols):
    smem = pl.BlockSpec(memory_space=pltpu.SMEM)
    hbm = pl.BlockSpec(memory_space=pl.ANY)
    vmem = pltpu.VMEM
    dma = pltpu.SemaphoreType.DMA
    shapes = (
        jax.ShapeDtypeStruct((PIX, 256), BF),
        jax.ShapeDtypeStruct((PIX, 512), BF),
        jax.ShapeDtypeStruct((32, 64), BF),
        jax.ShapeDtypeStruct((32, 64), BF),
        jax.ShapeDtypeStruct((32, 64), BF),
    )
    made = pl.pallas_call(
        kernel,
        out_shape=shapes,
        in_specs=[smem] + [pl.BlockSpec(memory_space=pltpu.HBM)] * 7,
        out_specs=(hbm,) * 5,
        scratch_shapes=[
            pltpu.SMEM((F,), jnp.int32),
            vmem((PIX, 256), BF), vmem((KEYS, 512), BF), vmem((PIX, 256), BF),
            vmem((2, 1024), BF), vmem((2, 2048), BF), vmem((1000, 256), F32),
            vmem((F, 2, 2, 128), BF), vmem((len(ROOTS), 2, F, 2, 128), BF), vmem((2, 2 * NZ, 32, 128), BF),
            vmem((2, 2, 2 * PIX, 128), BF), vmem((KEYS, 512), F32),
            vmem((2, HALO, 512), BF), vmem((2, HALO, 512), BF),
            vmem((TOK, 128), BF), vmem((TOK, 128), BF), vmem((80, TOK), BF), vmem((64, TOK), F32),
            vmem((16, TOK), F32), vmem((16, TOK), F32), vmem((16, TOK), F32), vmem((QT, 128), F32),
            vmem((PIX, 256), BF), vmem((PIX, 512), BF),
            vmem((32, 64), BF), vmem((32, 64), BF), vmem((32, 64), BF),
            dma((7,)), dma((5,)), dma((2,)), dma((2,)), dma((2,)), dma((2,)),
            dma((len(ROOTS), F)), dma((len(ROOTS), F)), dma,
            dma((NZ,)), dma((NZ,)), dma((NZ,)), dma((NZ,)),
        ],
        compiler_params=pltpu.CompilerParams(
            collective_id=0, has_side_effects=True, vmem_limit_bytes=24 * 1024 * 1024
        ),
    )(
        timesteps,
        *(
            pltpu.with_memory_space_constraint(x, pltpu.HBM)
            for x in (
                valid_cols,
                fine_q.reshape(PIX, 256), fine_kv.reshape(PIX, 512), cotangent.reshape(PIX, 256),
                coarse_q.reshape(2, 1024), coarse_kv.reshape(2, 2048), gain_table,
            )
        ),
    )
    dfq, dfkv, dq, dk, dv = pl.pallas_call(
        placing,
        out_shape=shapes,
        in_specs=[hbm] * 5,
        out_specs=(pl.BlockSpec(memory_space=pltpu.HBM),) * 5,
        scratch_shapes=[dma((5,))],
        compiler_params=pltpu.CompilerParams(vmem_limit_bytes=1024 * 1024),
    )(*made)
    return (
        dfq.reshape(1, 8, 16, 256), dfkv.reshape(1, 8, 16, 512),
        dq.reshape(F, 1, 2, 64), dk.reshape(F, 1, 2, 64), dv.reshape(F, 1, 2, 64),
    )


def solution(mesh):
    placed = P("frames", "rows", None, None)
    heads = P(None, "rows", None, "frames")
    return jax.shard_map(
        local,
        mesh=mesh,
        in_specs=(placed, placed, placed, placed, placed, P(), P("frames"), P()),
        out_specs=(placed, placed, heads, heads, heads),
        check_vma=False,
    )
```

```python
import functools

import jax
import jax.numpy as jnp
from jax import lax
from jax.experimental import pallas as pl
from jax.experimental.pallas import tpu as pltpu
from jax.sharding import PartitionSpec as P

F = 16
NZ = 32
ROWS = 64
HALO = 48
PIX = 128
KEYS = PIX + 2 * HALO
TOK = 2048
QT = 256
KT = 128
NEG = -1e30
BF = jnp.bfloat16
F32 = jnp.float32
MESH = pl.DeviceIdType.MESH


ROOTS = (0,)
SHARED = (16, 14, -14)


def tree():
    children = {0: [5, -5, 1, -1], 15: [16, 14], -15: [-14], 1: [2], -1: [-2]}
    for k in (5, -5, 10, -10):
        sign = 1 if k > 0 else -1
        hops = (5, -1, 1, -2, 2, 3) if abs(k) == 10 else (5, -1, 1)
        if abs(k) == 5:
            children[k + 1] = [k + 2]
            children[k - 1] = [k - 2]
        children[k] = [k + sign * h for h in hops]
    cost = {d: 4.4 + 0.6 * abs(d) for d in ROOTS}
    todo = list(ROOTS)
    while todo:
        d = todo.pop(0)
        for c in children.get(d, []):
            cost[c] = cost[d] + 2.0 + 0.6 * abs(c - d)
            todo.append(c)
    order = sorted((d for d in cost if d), key=lambda d: (cost[d], -d))
    return children, order


def dot(a, b, ca, cb):
    return lax.dot_general(a, b, (((ca,), (cb,)), ((), ())), preferred_element_type=F32)


def kernel(
    ts, vc_h, fq_h, fkv_h, cot_h, cq_h, ckv_h, gain_h,
    dfq_h, dfkv_h, dq_h, dk_h, dv_h,
    vc, fq, kv, cot, cq, ckv, gain, stage, land, buf,
    gs, dkv, rim_out, rim_in, a_ref, b_ref, t_ref, g_ref, top_ref, sum_ref, dot_ref, bias_ref,
    o_fq, o_fkv, o_q, o_k, o_v,
    in_sem, out_sem, halo_s, halo_r, rim_s, rim_r, a2a_s, a2a_r, self_sem,
    z_s, z_r, x_s, x_r,
):
    f = lax.axis_index("frames")
    r = lax.axis_index("rows")
    xl = r // NZ
    z = lax.rem(r, NZ)

    def zdev(d, head=f, column=xl):
        return (head, column * NZ + lax.rem(z + d + NZ, NZ))

    xdev = (f, (1 - xl) * NZ + z)
    above = (f, lax.rem(r + ROWS - 1, ROWS))
    below = (f, lax.rem(r + 1, ROWS))

    children, order = tree()
    slots = {d: 2 * i for i, d in enumerate([0] + order)}
    parent = {c: d for d, cs in children.items() for c in cs}

    loads = [
        pltpu.make_async_copy(src, dst, in_sem.at[i])
        for i, (src, dst) in enumerate(
            (
                (gain_h, gain),
                (cot_h, cot),
                (ckv_h, ckv),
                (cq_h, cq),
                (vc_h, vc),
                (fq_h, fq),
                (fkv_h, kv.at[pl.ds(HALO, PIX)]),
            )
        )
    ]
    barrier = pltpu.get_barrier_semaphore()
    hops = sorted({c - d for d, cs in children.items() for c in cs} | {d - c for d, cs in children.items() for c in cs})
    skew = sorted({s * (c - parent[c]) for c in SHARED for s in (1, -1)})
    peers = [zdev(o, lax.rem(f + k, F)) for o in ROOTS for k in range(F) if o or k]
    peers += [zdev(o) for o in hops] + [zdev(o, f, 1 - xl) for o in skew] + [xdev, above, below]
    for peer in peers:
        pl.semaphore_signal(barrier, inc=1, device_id=peer, device_id_type=MESH)

    for c in loads:
        c.start()

    for c in loads[:5]:
        c.wait()

    gain_row = gain[pl.ds(ts[0], 1), :]
    rows = []
    for a in range(2):
        t = cot[pl.ds(64 * a, 16), :].astype(F32)
        for i in range(1, 4):
            t = t + cot[pl.ds(64 * a + 16 * i, 16), :].astype(F32)
        rows.append([jnp.sum(t[4 * m : 4 * m + 4], axis=0, keepdims=True) * gain_row for m in range(4)])
    pooled = jnp.concatenate(
        [
            jnp.concatenate([rows[0][2 * c], rows[0][2 * c + 1], rows[1][2 * c], rows[1][2 * c + 1]], axis=1)
            for c in range(2)
        ],
        axis=0,
    )
    half = lax.broadcasted_iota(jnp.int32, (2, 1024), 1) % 128 < 64
    kv_all = ckv[...].astype(F32)
    for part, (one, two) in enumerate(((cq[...].astype(F32), kv_all[:, :1024]), (kv_all[:, 1024:], pooled))):
        even = jnp.where(half, one, pltpu.roll(two, 64, 1)).astype(BF)
        odd = jnp.where(half, pltpu.roll(one, 1024 - 64, 1), two).astype(BF)
        for j in range(8):
            stage[2 * j, part] = even[:, 128 * j : 128 * j + 128]
            stage[2 * j + 1, part] = odd[:, 128 * j : 128 * j + 128]

    pl.semaphore_wait(barrier, len(peers))

    def a2a(o, k):
        there = lax.rem(f + k, F)
        at = ROOTS.index(o)
        return pltpu.make_async_remote_copy(
            src_ref=stage.at[there], dst_ref=land.at[at, :, f],
            send_sem=a2a_s.at[at, k], recv_sem=a2a_r.at[at, k],
            device_id=zdev(o, there), device_id_type=MESH,
        )

    def a2a_in(o, k):
        here = lax.rem(f + F - k, F)
        at = ROOTS.index(o)
        return pltpu.make_async_remote_copy(
            src_ref=stage.at[here], dst_ref=land.at[at, :, here],
            send_sem=a2a_s.at[at, k], recv_sem=a2a_r.at[at, k],
            device_id=zdev(-o, here), device_id_type=MESH,
        )

    sends = [(o, k) for o in ROOTS for k in range(F) if o or k]
    own = pltpu.make_async_copy(stage.at[f], land.at[ROOTS.index(0), :, f], self_sem)
    own.start()
    for o, k in sends:
        a2a(o, k).start()

    halos = [
        pltpu.make_async_remote_copy(
            src_ref=fkv_h.at[pl.ds(PIX - HALO, HALO)], dst_ref=kv.at[pl.ds(0, HALO)],
            send_sem=halo_s.at[0], recv_sem=halo_r.at[0], device_id=below, device_id_type=MESH,
        ),
        pltpu.make_async_remote_copy(
            src_ref=fkv_h.at[pl.ds(0, HALO)], dst_ref=kv.at[pl.ds(HALO + PIX, HALO)],
            send_sem=halo_s.at[1], recv_sem=halo_r.at[1], device_id=above, device_id_type=MESH,
        ),
    ]
    for c in halos:
        c.start()

    def gather_heads(o):
        if o == 0:
            own.wait()
        for k in range(F):
            if o or k:
                a2a_in(o, k).wait_recv()
        for part in range(2):
            for i in range(F):
                buf[part, slots[o], 2 * i : 2 * i + 2, :] = land[ROOTS.index(o), part, i]

    def pass_z(d, c):
        return pltpu.make_async_remote_copy(
            src_ref=buf.at[:, slots[d]], dst_ref=buf.at[:, slots[c]],
            send_sem=z_s.at[c % NZ], recv_sem=z_r.at[c % NZ],
            device_id=zdev(c - d), device_id_type=MESH,
        )

    def pass_x(d):
        return pltpu.make_async_remote_copy(
            src_ref=buf.at[:, slots[d]], dst_ref=buf.at[:, slots[d] + 1],
            send_sem=x_s.at[d % NZ], recv_sem=x_r.at[d % NZ],
            device_id=xdev, device_id_type=MESH,
        )

    def pass_both(c):
        d = parent[c]
        return pltpu.make_async_remote_copy(
            src_ref=buf.at[:, slots[d]], dst_ref=buf.at[:, slots[c] + 1],
            send_sem=x_s.at[c % NZ], recv_sem=x_r.at[c % NZ],
            device_id=zdev(c - d, f, 1 - xl), device_id_type=MESH,
        )

    def other(d):
        return pass_both(d) if d in SHARED else pass_x(d)

    def hand_on(d):
        for c in children.get(d, []):
            pass_z(d, c).start()
            if c in SHARED:
                pass_both(c).start()
        if d not in SHARED:
            pass_x(d).start()

    def arrive(d):
        if d in ROOTS:
            gather_heads(d)
        else:
            pass_z(parent[d], d).wait_recv()
        hand_on(d)

    lane = lax.broadcasted_iota(jnp.int32, (PIX, 128), 1)

    def fine_prepare():
        for c in loads[5:]:
            c.wait()
        for c in halos:
            c.wait_recv()
        for p in range(2):
            cols = slice(128 * p, 128 * p + 128)
            q = fq[:, cols].astype(F32) * 0.125
            g = cot[:, cols].astype(F32) * gain_row[:, cols]
            for e in range(2):
                mine = lane < 64 if e == 0 else lane >= 64
                gs[0, p, pl.ds(PIX * e, PIX), :] = jnp.where(mine, q, 0.0).astype(BF)
                gs[1, p, pl.ds(PIX * e, PIX), :] = jnp.where(mine, g, 0.0).astype(BF)

    def fine_pair(p):
        qs = gs[0, p]
        g = gs[1, p]
        keys = kv[:, 128 * p : 128 * p + 128]
        values = kv[:, 256 + 128 * p : 256 + 128 * p + 128]
        qi = lax.broadcasted_iota(jnp.int32, (2 * PIX, KEYS), 0) % PIX
        ki = lax.broadcasted_iota(jnp.int32, (2 * PIX, KEYS), 1)
        dr = ki // 16 - 3 - qi // 16
        kc = ki % 16
        dc = kc - qi % 16
        row = r * 8 + ki // 16 - 3
        near = (jnp.abs(dr) <= 3) & (jnp.abs(dc) <= 3) & (row >= 0) & (row < ROWS * 8) & (kc < vc[f])
        near = near | ((dr == 0) & (dc == 0))
        s = jnp.where(near, dot(qs, keys, 1, 1), NEG)
        top = jnp.max(s, axis=1, keepdims=True)
        e = jnp.exp(s - top)
        w = e / jnp.sum(e, axis=1, keepdims=True)
        low = w.astype(BF)
        out = dot(low, values, 1, 0)
        row_dot = jnp.sum(g.astype(F32) * out, axis=1, keepdims=True)
        wg = dot(g, values, 1, 1)
        sg = (w * (wg - row_dot)).astype(BF)
        dq = dot(sg, keys, 1, 0) * 0.125
        o_fq[:, 128 * p : 128 * p + 128] = jnp.where(lane < 64, dq[:PIX], dq[PIX:]).astype(BF)
        dkv[:, 128 * p : 128 * p + 128] = dot(sg, qs, 0, 0)
        dkv[:, 256 + 128 * p : 256 + 128 * p + 128] = dot(low, g, 0, 0)

    rims = [
        pltpu.make_async_remote_copy(
            src_ref=rim_out.at[0], dst_ref=rim_in.at[0],
            send_sem=rim_s.at[0], recv_sem=rim_r.at[0], device_id=above, device_id_type=MESH,
        ),
        pltpu.make_async_remote_copy(
            src_ref=rim_out.at[1], dst_ref=rim_in.at[1],
            send_sem=rim_s.at[1], recv_sem=rim_r.at[1], device_id=below, device_id_type=MESH,
        ),
    ]
    fine_out = [
        pltpu.make_async_copy(o_fq, dfq_h, out_sem.at[0]),
        pltpu.make_async_copy(o_fkv, dfkv_h, out_sem.at[1]),
    ]

    def fine_send():
        rim_out[0] = dkv[pl.ds(0, HALO), :].astype(BF)
        rim_out[1] = dkv[pl.ds(HALO + PIX, HALO), :].astype(BF)
        for c in rims:
            c.start()
        fine_out[0].start()

    def fine_finish():
        for c in rims:
            c.wait_recv()
        mid = PIX - 2 * HALO
        o_fkv[pl.ds(0, HALO), :] = (dkv[pl.ds(HALO, HALO), :] + rim_in[1].astype(F32)).astype(BF)
        o_fkv[pl.ds(HALO, mid), :] = dkv[pl.ds(2 * HALO, mid), :].astype(BF)
        o_fkv[pl.ds(HALO + mid, HALO), :] = (
            dkv[pl.ds(2 * HALO + mid, HALO), :] + rim_in[0].astype(F32)
        ).astype(BF)
        fine_out[1].start()

    tl = lax.broadcasted_iota(jnp.int32, (32, 128), 1)
    ti = lax.broadcasted_iota(jnp.int32, (32, 128), 0)

    def coarse_prepare():
        limit = jnp.zeros((32, 128), jnp.int32)
        for i in range(F):
            limit = jnp.where(ti // 2 == i, vc[i], limit)
        bias = jnp.where((tl == 0) & ((ti % 2) * 8 >= limit), NEG, 0.0).astype(F32)
        bias_ref[...] = jnp.broadcast_to(bias[None], (8, 32, 128)).reshape(QT, 128)
        t_ref[pl.ds(64, 16), :] = jnp.ones((16, TOK), BF)

    def score(q, c):
        return dot(a_ref[pl.ds(KT * c, KT), :], b_ref[pl.ds(QT * q, QT), :], 1, 1)

    def weigh(q, c, s):
        top = jnp.max(s, axis=0, keepdims=True)
        top_ref[c : c + 1, pl.ds(QT * q, QT)] = top
        return dot(t_ref[:, pl.ds(KT * c, KT)], jnp.exp(s - top).astype(BF), 1, 0)

    def settle(q, c, out):
        qs = pl.ds(QT * q, QT)
        sum_ref[c : c + 1, qs] = out[64:65]
        dot_ref[c : c + 1, qs] = jnp.sum(out[:64] * g_ref[:, qs], axis=0, keepdims=True)

    def parts(todo):
        depth = 8
        scores = [score(*p) for p in todo[:depth]]
        outs = []
        for i, p in enumerate(todo):
            if i + depth < len(todo):
                scores.append(score(*todo[i + depth]))
            outs.append(weigh(*p, scores[i]))
            if i >= depth:
                settle(*todo[i - depth], outs[i - depth])
        for i in range(max(0, len(todo) - depth), len(todo)):
            settle(*todo[i], outs[i])

    def coarse_tile(t):
        for d in ([0] + order)[4 * t : 4 * t + 4]:
            other(d).wait_recv()
        at = pl.ds(QT * t, QT)
        upper = lax.broadcasted_iota(jnp.int32, (QT, 128), 1) >= 64
        unit = (lax.broadcasted_iota(jnp.int32, (QT, 128), 1) == 0).astype(F32)
        qk = buf[0, 8 * t : 8 * t + 8].reshape(QT, 128).astype(F32)
        a_ref[at, :] = jnp.where(upper, qk * 0.125, bias_ref[...]).astype(BF)
        b_ref[at, :] = jnp.where(upper, pltpu.roll(qk, 64, 1), unit).astype(BF)
        vg = jnp.transpose(buf[1, 8 * t : 8 * t + 8].reshape(QT, 128).astype(F32), (1, 0))
        t_ref[pl.ds(0, 64), at] = vg[:64].astype(BF)
        g_ref[:, at] = vg[64:]
        parts([(i, c) for i in range(t) for c in (2 * t, 2 * t + 1)] + [(t, c) for c in range(2 * t + 2)])

    def tiles(*ts_):
        return [functools.partial(coarse_tile, t) for t in ts_]

    work = {
        2: [coarse_prepare],
        -5: [fine_prepare, functools.partial(fine_pair, 0), functools.partial(fine_pair, 1), fine_send],
        -10: tiles(0, 1, 2) + [fine_finish],
        -15: tiles(3, 4, 5),
    }

    for d in [0] + order:
        arrive(d)
        for piece in work.get(d, []):
            piece()
    coarse_tile(6)
    coarse_tile(7)

    top = jnp.max(top_ref[...], axis=0, keepdims=True)
    share = jnp.exp(top_ref[...] - top)
    total = jnp.sum(share * sum_ref[...], axis=0, keepdims=True)
    log_total = top + jnp.log(total)
    dots = jnp.sum(share * dot_ref[...], axis=0, keepdims=True) / total

    qk = buf[0].reshape(TOK, 128)
    vg = buf[1].reshape(TOK, 128)
    mine = buf[1, 0].astype(F32)
    v_own = mine[:, :64].astype(BF)
    g_wide = pltpu.roll(mine, 64, 1)[:, :64]

    s = dot(a_ref[0:32, :], b_ref[...], 1, 1)
    w = jnp.exp(s - log_total)
    dw = dot(v_own, g_ref[...].astype(BF), 1, 0)
    sg = (w * (dw - dots)).astype(BF)
    o_v[...] = dot(w.astype(BF), vg, 1, 0)[:, 64:].astype(BF)
    o_k[...] = (dot(sg, qk, 1, 0)[:, :64] * 0.125).astype(BF)

    s = dot(b_ref[0:32, :], a_ref[...], 1, 1)
    top = jnp.max(s, axis=1, keepdims=True)
    e = jnp.exp(s - top)
    w = e / jnp.sum(e, axis=1, keepdims=True)
    out = dot(w.astype(BF), vg, 1, 0)[:, :64]
    row_dot = jnp.sum(g_wide * out, axis=1, keepdims=True)
    dw = dot(g_wide.astype(BF), t_ref[pl.ds(0, 64), :], 1, 0)
    sg = (w * (dw - row_dot)).astype(BF)
    o_q[...] = (dot(sg, qk, 1, 0)[:, 64:] * 0.125).astype(BF)

    outs = [
        pltpu.make_async_copy(o_q, dq_h, out_sem.at[2]),
        pltpu.make_async_copy(o_k, dk_h, out_sem.at[3]),
        pltpu.make_async_copy(o_v, dv_h, out_sem.at[4]),
    ]
    for c in outs:
        c.start()
    for o, k in sends:
        a2a(o, k).wait_send()
    for c in halos + rims:
        c.wait_send()
    for d in [0] + order:
        if d not in ROOTS:
            pass_z(parent[d], d).wait_send()
        other(d).wait_send()
    for c in fine_out + outs:
        c.wait()


def placing(*refs):
    sem = refs[-1]
    copies = [pltpu.make_async_copy(refs[i], refs[5 + i], sem.at[i]) for i in range(5)]
    for c in copies:
        c.start()
    for c in copies:
        c.wait()


def local(fine_q, fine_kv, coarse_q, coarse_kv, cotangent, gain_table, timesteps, valid_cols):
    smem = pl.BlockSpec(memory_space=pltpu.SMEM)
    hbm = pl.BlockSpec(memory_space=pl.ANY)
    vmem = pltpu.VMEM
    dma = pltpu.SemaphoreType.DMA
    shapes = (
        jax.ShapeDtypeStruct((PIX, 256), BF),
        jax.ShapeDtypeStruct((PIX, 512), BF),
        jax.ShapeDtypeStruct((32, 64), BF),
        jax.ShapeDtypeStruct((32, 64), BF),
        jax.ShapeDtypeStruct((32, 64), BF),
    )
    made = pl.pallas_call(
        kernel,
        out_shape=shapes,
        in_specs=[smem] + [pl.BlockSpec(memory_space=pltpu.HBM)] * 7,
        out_specs=(hbm,) * 5,
        scratch_shapes=[
            pltpu.SMEM((F,), jnp.int32),
            vmem((PIX, 256), BF), vmem((KEYS, 512), BF), vmem((PIX, 256), BF),
            vmem((2, 1024), BF), vmem((2, 2048), BF), vmem((1000, 256), F32),
            vmem((F, 2, 2, 128), BF), vmem((len(ROOTS), 2, F, 2, 128), BF), vmem((2, 2 * NZ, 32, 128), BF),
            vmem((2, 2, 2 * PIX, 128), BF), vmem((KEYS, 512), F32),
            vmem((2, HALO, 512), BF), vmem((2, HALO, 512), BF),
            vmem((TOK, 128), BF), vmem((TOK, 128), BF), vmem((80, TOK), BF), vmem((64, TOK), F32),
            vmem((16, TOK), F32), vmem((16, TOK), F32), vmem((16, TOK), F32), vmem((QT, 128), F32),
            vmem((PIX, 256), BF), vmem((PIX, 512), BF),
            vmem((32, 64), BF), vmem((32, 64), BF), vmem((32, 64), BF),
            dma((7,)), dma((5,)), dma((2,)), dma((2,)), dma((2,)), dma((2,)),
            dma((len(ROOTS), F)), dma((len(ROOTS), F)), dma,
            dma((NZ,)), dma((NZ,)), dma((NZ,)), dma((NZ,)),
        ],
        compiler_params=pltpu.CompilerParams(
            collective_id=0, has_side_effects=True, vmem_limit_bytes=24 * 1024 * 1024
        ),
    )(
        timesteps,
        *(
            pltpu.with_memory_space_constraint(x, pltpu.HBM)
            for x in (
                valid_cols,
                fine_q.reshape(PIX, 256), fine_kv.reshape(PIX, 512), cotangent.reshape(PIX, 256),
                coarse_q.reshape(2, 1024), coarse_kv.reshape(2, 2048), gain_table,
            )
        ),
    )
    dfq, dfkv, dq, dk, dv = pl.pallas_call(
        placing,
        out_shape=shapes,
        in_specs=[hbm] * 5,
        out_specs=(pl.BlockSpec(memory_space=pltpu.HBM),) * 5,
        scratch_shapes=[dma((5,))],
        compiler_params=pltpu.CompilerParams(vmem_limit_bytes=1024 * 1024),
    )(*made)
    return (
        dfq.reshape(1, 8, 16, 256), dfkv.reshape(1, 8, 16, 512),
        dq.reshape(F, 1, 2, 64), dk.reshape(F, 1, 2, 64), dv.reshape(F, 1, 2, 64),
    )


def solution(mesh):
    placed = P("frames", "rows", None, None)
    heads = P(None, "rows", None, "frames")
    return jax.shard_map(
        local,
        mesh=mesh,
        in_specs=(placed, placed, placed, placed, placed, P(), P("frames"), P()),
        out_specs=(placed, placed, heads, heads, heads),
        check_vma=False,
    )
```

```python
import functools

import jax
import jax.numpy as jnp
from jax import lax
from jax.experimental import pallas as pl
from jax.experimental.pallas import tpu as pltpu
from jax.sharding import PartitionSpec as P

F = 16
NZ = 32
ROWS = 64
HALO = 48
PIX = 128
KEYS = PIX + 2 * HALO
TOK = 2048
QT = 256
KT = 128
NEG = -1e30
BF = jnp.bfloat16
F32 = jnp.float32
MESH = pl.DeviceIdType.MESH


ROOTS = (0,)
SHARED = (16, 14, -14)


def tree():
    children = {0: [5, -5, 1, -1], 15: [16, 14], -15: [-14], 1: [2], -1: [-2]}
    for k in (5, -5, 10, -10):
        sign = 1 if k > 0 else -1
        hops = (5, -1, 1, -2, 2, 3) if abs(k) == 10 else (5, -1, 1)
        if abs(k) == 5:
            children[k + 1] = [k + 2]
            children[k - 1] = [k - 2]
        children[k] = [k + sign * h for h in hops]
    cost = {d: 4.4 + 0.6 * abs(d) for d in ROOTS}
    todo = list(ROOTS)
    while todo:
        d = todo.pop(0)
        for c in children.get(d, []):
            cost[c] = cost[d] + 2.0 + 0.6 * abs(c - d)
            todo.append(c)
    order = sorted((d for d in cost if d), key=lambda d: (cost[d], -d))
    return children, order


def dot(a, b, ca, cb):
    return lax.dot_general(a, b, (((ca,), (cb,)), ((), ())), preferred_element_type=F32)


def kernel(
    ts, vc_h, fq_h, fkv_h, cot_h, cq_h, ckv_h, gain_h,
    dfq_h, dfkv_h, dq_h, dk_h, dv_h,
    vc, fq, kv, cot, cq, ckv, gain, stage, land, buf,
    gs, dkv, rim_out, rim_in, a_ref, b_ref, t_ref, g_ref, top_ref, sum_ref, dot_ref, bias_ref,
    o_fq, o_fkv, o_q, o_k, o_v,
    in_sem, out_sem, halo_s, halo_r, rim_s, rim_r, a2a_s, a2a_r, self_sem,
    z_s, z_r, x_s, x_r,
):
    f = lax.axis_index("frames")
    r = lax.axis_index("rows")
    xl = r // NZ
    z = lax.rem(r, NZ)

    def zdev(d, head=f, column=xl):
        return (head, column * NZ + lax.rem(z + d + NZ, NZ))

    xdev = (f, (1 - xl) * NZ + z)
    above = (f, lax.rem(r + ROWS - 1, ROWS))
    below = (f, lax.rem(r + 1, ROWS))

    children, order = tree()
    slots = {d: 2 * i for i, d in enumerate([0] + order)}
    parent = {c: d for d, cs in children.items() for c in cs}

    loads = [
        pltpu.make_async_copy(src, dst, in_sem.at[i])
        for i, (src, dst) in enumerate(
            (
                (gain_h, gain),
                (cot_h, cot),
                (ckv_h, ckv),
                (cq_h, cq),
                (vc_h, vc),
                (fq_h, fq),
                (fkv_h, kv.at[pl.ds(HALO, PIX)]),
            )
        )
    ]
    barrier = pltpu.get_barrier_semaphore()
    hops = sorted({c - d for d, cs in children.items() for c in cs} | {d - c for d, cs in children.items() for c in cs})
    skew = sorted({s * (c - parent[c]) for c in SHARED for s in (1, -1)})
    peers = [zdev(o, lax.rem(f + k, F)) for o in ROOTS for k in range(F) if o or k]
    peers += [zdev(o) for o in hops] + [zdev(o, f, 1 - xl) for o in skew] + [xdev, above, below]
    for peer in peers:
        pl.semaphore_signal(barrier, inc=1, device_id=peer, device_id_type=MESH)

    for c in loads:
        c.start()

    for c in loads[:5]:
        c.wait()

    gain_row = gain[pl.ds(ts[0], 1), :]
    rows = []
    for a in range(2):
        t = cot[pl.ds(64 * a, 16), :].astype(F32)
        for i in range(1, 4):
            t = t + cot[pl.ds(64 * a + 16 * i, 16), :].astype(F32)
        rows.append([jnp.sum(t[4 * m : 4 * m + 4], axis=0, keepdims=True) * gain_row for m in range(4)])
    pooled = jnp.concatenate(
        [
            jnp.concatenate([rows[0][2 * c], rows[0][2 * c + 1], rows[1][2 * c], rows[1][2 * c + 1]], axis=1)
            for c in range(2)
        ],
        axis=0,
    )
    half = lax.broadcasted_iota(jnp.int32, (2, 1024), 1) % 128 < 64
    kv_all = ckv[...].astype(F32)
    for part, (one, two) in enumerate(((cq[...].astype(F32), kv_all[:, :1024]), (kv_all[:, 1024:], pooled))):
        even = jnp.where(half, one, pltpu.roll(two, 64, 1)).astype(BF)
        odd = jnp.where(half, pltpu.roll(one, 1024 - 64, 1), two).astype(BF)
        for j in range(8):
            stage[2 * j, part] = even[:, 128 * j : 128 * j + 128]
            stage[2 * j + 1, part] = odd[:, 128 * j : 128 * j + 128]

    pl.semaphore_wait(barrier, len(peers))

    def a2a(o, k):
        there = lax.rem(f + k, F)
        at = ROOTS.index(o)
        return pltpu.make_async_remote_copy(
            src_ref=stage.at[there], dst_ref=land.at[at, :, f],
            send_sem=a2a_s.at[at, k], recv_sem=a2a_r.at[at, k],
            device_id=zdev(o, there), device_id_type=MESH,
        )

    def a2a_in(o, k):
        here = lax.rem(f + F - k, F)
        at = ROOTS.index(o)
        return pltpu.make_async_remote_copy(
            src_ref=stage.at[here], dst_ref=land.at[at, :, here],
            send_sem=a2a_s.at[at, k], recv_sem=a2a_r.at[at, k],
            device_id=zdev(-o, here), device_id_type=MESH,
        )

    sends = [(o, k) for o in ROOTS for k in range(F) if o or k]
    own = pltpu.make_async_copy(stage.at[f], land.at[ROOTS.index(0), :, f], self_sem)
    own.start()
    for o, k in sends:
        a2a(o, k).start()

    halos = [
        pltpu.make_async_remote_copy(
            src_ref=fkv_h.at[pl.ds(PIX - HALO, HALO)], dst_ref=kv.at[pl.ds(0, HALO)],
            send_sem=halo_s.at[0], recv_sem=halo_r.at[0], device_id=below, device_id_type=MESH,
        ),
        pltpu.make_async_remote_copy(
            src_ref=fkv_h.at[pl.ds(0, HALO)], dst_ref=kv.at[pl.ds(HALO + PIX, HALO)],
            send_sem=halo_s.at[1], recv_sem=halo_r.at[1], device_id=above, device_id_type=MESH,
        ),
    ]
    for c in halos:
        c.start()

    def gather_heads(o):
        if o == 0:
            own.wait()
        for k in range(F):
            if o or k:
                a2a_in(o, k).wait_recv()
        for part in range(2):
            for i in range(F):
                buf[part, slots[o], 2 * i : 2 * i + 2, :] = land[ROOTS.index(o), part, i]

    def pass_z(d, c):
        return pltpu.make_async_remote_copy(
            src_ref=buf.at[:, slots[d]], dst_ref=buf.at[:, slots[c]],
            send_sem=z_s.at[c % NZ], recv_sem=z_r.at[c % NZ],
            device_id=zdev(c - d), device_id_type=MESH,
        )

    def pass_x(d):
        return pltpu.make_async_remote_copy(
            src_ref=buf.at[:, slots[d]], dst_ref=buf.at[:, slots[d] + 1],
            send_sem=x_s.at[d % NZ], recv_sem=x_r.at[d % NZ],
            device_id=xdev, device_id_type=MESH,
        )

    def pass_both(c):
        d = parent[c]
        return pltpu.make_async_remote_copy(
            src_ref=buf.at[:, slots[d]], dst_ref=buf.at[:, slots[c] + 1],
            send_sem=x_s.at[c % NZ], recv_sem=x_r.at[c % NZ],
            device_id=zdev(c - d, f, 1 - xl), device_id_type=MESH,
        )

    def other(d):
        return pass_both(d) if d in SHARED else pass_x(d)

    def hand_on(d):
        for c in children.get(d, []):
            if c in SHARED:
                pass_both(c).start()
            pass_z(d, c).start()
        if d not in SHARED:
            pass_x(d).start()

    def arrive(d):
        if d in ROOTS:
            gather_heads(d)
        else:
            pass_z(parent[d], d).wait_recv()
        hand_on(d)

    lane = lax.broadcasted_iota(jnp.int32, (PIX, 128), 1)

    def fine_prepare():
        for c in loads[5:]:
            c.wait()
        for c in halos:
            c.wait_recv()
        for p in range(2):
            cols = slice(128 * p, 128 * p + 128)
            q = fq[:, cols].astype(F32) * 0.125
            g = cot[:, cols].astype(F32) * gain_row[:, cols]
            for e in range(2):
                mine = lane < 64 if e == 0 else lane >= 64
                gs[0, p, pl.ds(PIX * e, PIX), :] = jnp.where(mine, q, 0.0).astype(BF)
                gs[1, p, pl.ds(PIX * e, PIX), :] = jnp.where(mine, g, 0.0).astype(BF)

    def fine_pair(p):
        qs = gs[0, p]
        g = gs[1, p]
        keys = kv[:, 128 * p : 128 * p + 128]
        values = kv[:, 256 + 128 * p : 256 + 128 * p + 128]
        qi = lax.broadcasted_iota(jnp.int32, (2 * PIX, KEYS), 0) % PIX
        ki = lax.broadcasted_iota(jnp.int32, (2 * PIX, KEYS), 1)
        dr = ki // 16 - 3 - qi // 16
        kc = ki % 16
        dc = kc - qi % 16
        row = r * 8 + ki // 16 - 3
        near = (jnp.abs(dr) <= 3) & (jnp.abs(dc) <= 3) & (row >= 0) & (row < ROWS * 8) & (kc < vc[f])
        near = near | ((dr == 0) & (dc == 0))
        s = jnp.where(near, dot(qs, keys, 1, 1), NEG)
        top = jnp.max(s, axis=1, keepdims=True)
        e = jnp.exp(s - top)
        w = e / jnp.sum(e, axis=1, keepdims=True)
        low = w.astype(BF)
        out = dot(low, values, 1, 0)
        row_dot = jnp.sum(g.astype(F32) * out, axis=1, keepdims=True)
        wg = dot(g, values, 1, 1)
        sg = (w * (wg - row_dot)).astype(BF)
        dq = dot(sg, keys, 1, 0) * 0.125
        o_fq[:, 128 * p : 128 * p + 128] = jnp.where(lane < 64, dq[:PIX], dq[PIX:]).astype(BF)
        dkv[:, 128 * p : 128 * p + 128] = dot(sg, qs, 0, 0)
        dkv[:, 256 + 128 * p : 256 + 128 * p + 128] = dot(low, g, 0, 0)

    rims = [
        pltpu.make_async_remote_copy(
            src_ref=rim_out.at[0], dst_ref=rim_in.at[0],
            send_sem=rim_s.at[0], recv_sem=rim_r.at[0], device_id=above, device_id_type=MESH,
        ),
        pltpu.make_async_remote_copy(
            src_ref=rim_out.at[1], dst_ref=rim_in.at[1],
            send_sem=rim_s.at[1], recv_sem=rim_r.at[1], device_id=below, device_id_type=MESH,
        ),
    ]
    fine_out = [
        pltpu.make_async_copy(o_fq, dfq_h, out_sem.at[0]),
        pltpu.make_async_copy(o_fkv, dfkv_h, out_sem.at[1]),
    ]

    def fine_send():
        rim_out[0] = dkv[pl.ds(0, HALO), :].astype(BF)
        rim_out[1] = dkv[pl.ds(HALO + PIX, HALO), :].astype(BF)
        for c in rims:
            c.start()
        fine_out[0].start()

    def fine_finish():
        for c in rims:
            c.wait_recv()
        mid = PIX - 2 * HALO
        o_fkv[pl.ds(0, HALO), :] = (dkv[pl.ds(HALO, HALO), :] + rim_in[1].astype(F32)).astype(BF)
        o_fkv[pl.ds(HALO, mid), :] = dkv[pl.ds(2 * HALO, mid), :].astype(BF)
        o_fkv[pl.ds(HALO + mid, HALO), :] = (
            dkv[pl.ds(2 * HALO + mid, HALO), :] + rim_in[0].astype(F32)
        ).astype(BF)
        fine_out[1].start()

    tl = lax.broadcasted_iota(jnp.int32, (32, 128), 1)
    ti = lax.broadcasted_iota(jnp.int32, (32, 128), 0)

    def coarse_prepare():
        limit = jnp.zeros((32, 128), jnp.int32)
        for i in range(F):
            limit = jnp.where(ti // 2 == i, vc[i], limit)
        bias = jnp.where((tl == 0) & ((ti % 2) * 8 >= limit), NEG, 0.0).astype(F32)
        bias_ref[...] = jnp.broadcast_to(bias[None], (8, 32, 128)).reshape(QT, 128)
        t_ref[pl.ds(64, 16), :] = jnp.ones((16, TOK), BF)

    def score(q, c):
        return dot(a_ref[pl.ds(KT * c, KT), :], b_ref[pl.ds(QT * q, QT), :], 1, 1)

    def weigh(q, c, s):
        top = jnp.max(s, axis=0, keepdims=True)
        top_ref[c : c + 1, pl.ds(QT * q, QT)] = top
        return dot(t_ref[:, pl.ds(KT * c, KT)], jnp.exp(s - top).astype(BF), 1, 0)

    def settle(q, c, out):
        qs = pl.ds(QT * q, QT)
        sum_ref[c : c + 1, qs] = out[64:65]
        dot_ref[c : c + 1, qs] = jnp.sum(out[:64] * g_ref[:, qs], axis=0, keepdims=True)

    def parts(todo):
        depth = 8
        scores = [score(*p) for p in todo[:depth]]
        outs = []
        for i, p in enumerate(todo):
            if i + depth < len(todo):
                scores.append(score(*todo[i + depth]))
            outs.append(weigh(*p, scores[i]))
            if i >= depth:
                settle(*todo[i - depth], outs[i - depth])
        for i in range(max(0, len(todo) - depth), len(todo)):
            settle(*todo[i], outs[i])

    def coarse_tile(t):
        for d in ([0] + order)[4 * t : 4 * t + 4]:
            other(d).wait_recv()
        at = pl.ds(QT * t, QT)
        upper = lax.broadcasted_iota(jnp.int32, (QT, 128), 1) >= 64
        unit = (lax.broadcasted_iota(jnp.int32, (QT, 128), 1) == 0).astype(F32)
        qk = buf[0, 8 * t : 8 * t + 8].reshape(QT, 128).astype(F32)
        a_ref[at, :] = jnp.where(upper, qk * 0.125, bias_ref[...]).astype(BF)
        b_ref[at, :] = jnp.where(upper, pltpu.roll(qk, 64, 1), unit).astype(BF)
        vg = jnp.transpose(buf[1, 8 * t : 8 * t + 8].reshape(QT, 128).astype(F32), (1, 0))
        t_ref[pl.ds(0, 64), at] = vg[:64].astype(BF)
        g_ref[:, at] = vg[64:]
        parts([(i, c) for i in range(t) for c in (2 * t, 2 * t + 1)] + [(t, c) for c in range(2 * t + 2)])

    def tiles(*ts_):
        return [functools.partial(coarse_tile, t) for t in ts_]

    work = {
        2: [coarse_prepare],
        -5: [fine_prepare, functools.partial(fine_pair, 0), functools.partial(fine_pair, 1), fine_send],
        -10: tiles(0, 1, 2) + [fine_finish],
        -15: tiles(3, 4, 5),
    }

    for d in [0] + order:
        arrive(d)
        for piece in work.get(d, []):
            piece()
    coarse_tile(6)
    coarse_tile(7)

    top = jnp.max(top_ref[...], axis=0, keepdims=True)
    share = jnp.exp(top_ref[...] - top)
    total = jnp.sum(share * sum_ref[...], axis=0, keepdims=True)
    log_total = top + jnp.log(total)
    dots = jnp.sum(share * dot_ref[...], axis=0, keepdims=True) / total

    qk = buf[0].reshape(TOK, 128)
    vg = buf[1].reshape(TOK, 128)
    mine = buf[1, 0].astype(F32)
    v_own = mine[:, :64].astype(BF)
    g_wide = pltpu.roll(mine, 64, 1)[:, :64]

    s = dot(a_ref[0:32, :], b_ref[...], 1, 1)
    w = jnp.exp(s - log_total)
    dw = dot(v_own, g_ref[...].astype(BF), 1, 0)
    sg = (w * (dw - dots)).astype(BF)
    o_v[...] = dot(w.astype(BF), vg, 1, 0)[:, 64:].astype(BF)
    o_k[...] = (dot(sg, qk, 1, 0)[:, :64] * 0.125).astype(BF)

    s = dot(b_ref[0:32, :], a_ref[...], 1, 1)
    top = jnp.max(s, axis=1, keepdims=True)
    e = jnp.exp(s - top)
    w = e / jnp.sum(e, axis=1, keepdims=True)
    out = dot(w.astype(BF), vg, 1, 0)[:, :64]
    row_dot = jnp.sum(g_wide * out, axis=1, keepdims=True)
    dw = dot(g_wide.astype(BF), t_ref[pl.ds(0, 64), :], 1, 0)
    sg = (w * (dw - row_dot)).astype(BF)
    o_q[...] = (dot(sg, qk, 1, 0)[:, 64:] * 0.125).astype(BF)

    outs = [
        pltpu.make_async_copy(o_q, dq_h, out_sem.at[2]),
        pltpu.make_async_copy(o_k, dk_h, out_sem.at[3]),
        pltpu.make_async_copy(o_v, dv_h, out_sem.at[4]),
    ]
    for c in outs:
        c.start()
    for o, k in sends:
        a2a(o, k).wait_send()
    for c in halos + rims:
        c.wait_send()
    for d in [0] + order:
        if d not in ROOTS:
            pass_z(parent[d], d).wait_send()
        other(d).wait_send()
    for c in fine_out + outs:
        c.wait()


def placing(*refs):
    sem = refs[-1]
    copies = [pltpu.make_async_copy(refs[i], refs[5 + i], sem.at[i]) for i in range(5)]
    for c in copies:
        c.start()
    for c in copies:
        c.wait()


def local(fine_q, fine_kv, coarse_q, coarse_kv, cotangent, gain_table, timesteps, valid_cols):
    smem = pl.BlockSpec(memory_space=pltpu.SMEM)
    hbm = pl.BlockSpec(memory_space=pl.ANY)
    vmem = pltpu.VMEM
    dma = pltpu.SemaphoreType.DMA
    shapes = (
        jax.ShapeDtypeStruct((PIX, 256), BF),
        jax.ShapeDtypeStruct((PIX, 512), BF),
        jax.ShapeDtypeStruct((32, 64), BF),
        jax.ShapeDtypeStruct((32, 64), BF),
        jax.ShapeDtypeStruct((32, 64), BF),
    )
    made = pl.pallas_call(
        kernel,
        out_shape=shapes,
        in_specs=[smem] + [pl.BlockSpec(memory_space=pltpu.HBM)] * 7,
        out_specs=(hbm,) * 5,
        scratch_shapes=[
            pltpu.SMEM((F,), jnp.int32),
            vmem((PIX, 256), BF), vmem((KEYS, 512), BF), vmem((PIX, 256), BF),
            vmem((2, 1024), BF), vmem((2, 2048), BF), vmem((1000, 256), F32),
            vmem((F, 2, 2, 128), BF), vmem((len(ROOTS), 2, F, 2, 128), BF), vmem((2, 2 * NZ, 32, 128), BF),
            vmem((2, 2, 2 * PIX, 128), BF), vmem((KEYS, 512), F32),
            vmem((2, HALO, 512), BF), vmem((2, HALO, 512), BF),
            vmem((TOK, 128), BF), vmem((TOK, 128), BF), vmem((80, TOK), BF), vmem((64, TOK), F32),
            vmem((16, TOK), F32), vmem((16, TOK), F32), vmem((16, TOK), F32), vmem((QT, 128), F32),
            vmem((PIX, 256), BF), vmem((PIX, 512), BF),
            vmem((32, 64), BF), vmem((32, 64), BF), vmem((32, 64), BF),
            dma((7,)), dma((5,)), dma((2,)), dma((2,)), dma((2,)), dma((2,)),
            dma((len(ROOTS), F)), dma((len(ROOTS), F)), dma,
            dma((NZ,)), dma((NZ,)), dma((NZ,)), dma((NZ,)),
        ],
        compiler_params=pltpu.CompilerParams(
            collective_id=0, has_side_effects=True, vmem_limit_bytes=24 * 1024 * 1024
        ),
    )(
        timesteps,
        *(
            pltpu.with_memory_space_constraint(x, pltpu.HBM)
            for x in (
                valid_cols,
                fine_q.reshape(PIX, 256), fine_kv.reshape(PIX, 512), cotangent.reshape(PIX, 256),
                coarse_q.reshape(2, 1024), coarse_kv.reshape(2, 2048), gain_table,
            )
        ),
    )
    dfq, dfkv, dq, dk, dv = pl.pallas_call(
        placing,
        out_shape=shapes,
        in_specs=[hbm] * 5,
        out_specs=(pl.BlockSpec(memory_space=pltpu.HBM),) * 5,
        scratch_shapes=[dma((5,))],
        compiler_params=pltpu.CompilerParams(vmem_limit_bytes=1024 * 1024),
    )(*made)
    return (
        dfq.reshape(1, 8, 16, 256), dfkv.reshape(1, 8, 16, 512),
        dq.reshape(F, 1, 2, 64), dk.reshape(F, 1, 2, 64), dv.reshape(F, 1, 2, 64),
    )


def solution(mesh):
    placed = P("frames", "rows", None, None)
    heads = P(None, "rows", None, "frames")
    return jax.shard_map(
        local,
        mesh=mesh,
        in_specs=(placed, placed, placed, placed, placed, P(), P("frames"), P()),
        out_specs=(placed, placed, heads, heads, heads),
        check_vma=False,
    )
```
